256 devices in a mesh: dom: 64 (over x, z, core), sub: 4 (over y).
Axes of the slice: x: 4, y: 4, z: 8, core: 2. Of those that a mesh axis runs over, the one named last changes fastest.
Arguments:
- initial_state: float32 [320, 65536], P(None, ('dom', 'sub')), may hold values from -6 to 6
- cotangent: float32 [320, 65536], P(None, ('dom', 'sub')), may hold values from -6 to 6
- volume_operator: bfloat16 [320, 320], replicated, may hold values from -0.3125 to 0.3125
- in_weight: bfloat16 [64, 10], replicated, may hold values from -2 to 2
- in_bias: float32 [64], replicated, may hold values from -3 to 3
- mid_weight: bfloat16 [64, 64], replicated, may hold values from -0.75 to 0.75
- mid_bias: float32 [64], replicated, may hold values from -3 to 3
- out_weight: bfloat16 [5, 64], replicated, may hold values from -0.75 to 0.75
- flux_matrix: float32 [5, 5], replicated, may hold values from -2.5 to 2.5
- dom_send: int32 [64, 1024], P('dom', 'sub'), may hold values from 0 to 1535
- dom_count: int32 [64, 32], P('dom', 'sub'), may hold values from 0 to 32, as said below
- sub_send: int32 [64, 2048], P('dom', 'sub'), may hold values from 0 to 1535
- partner: int32 [64, 6144], P('dom', 'sub'), may hold values from 0 to 2303, as said below
Outputs:
- final_state: float32 [320, 65536], P(None, ('dom', 'sub'))
- adjoint_state: float32 [320, 65536], P(None, ('dom', 'sub'))
The draws below stay inside these ranges and needn't reach their ends.
Inputs may be any that keep to these rules, and one draw needn't show every extreme that they name: `dom_send`: local face slots, face*256+element. `dom_count`: counts of live slots; in every partition some block is full. `sub_send`: local face slots, face*256+element. `partner`: entries below 1536 name a local face slot; each received slot 6*256+r is named by exactly one face of the partition.
All inputs are finite; a program needn't handle non-finite values.
Results may differ from the reference program's by a relative error of at most 0.0033.
Values may be sent and summed in bfloat16 or wider, within the bound.
No kernel may reach another device: no remote copies, remote signals or barrier semaphores. Data moves between devices by JAX's collectives and lax.ppermute only.
A program may use at most 64 MiB of HBM per device.

```python
import jax
import jax.numpy as jnp
import numpy as np
from jax import lax

VARS = 5
HIDDEN_SIZE = 64
REACH = 4
PEER_SLOTS = 32
SUB_SLOTS = 128
E_DEV = 256
ROWS = 320
ELEMS = 65536
SOURCES = 768
N_DOM = 64
N_SUB = 4


def draw_dom_count(key, part):
    devices = N_DOM * N_SUB
    pair_count = 2 * REACH
    key_one, key_two, key_three = jax.random.split(jax.random.fold_in(key, 11), 3)
    load_level = jax.random.randint(key_one, (devices, 1), 1, 5)
    counts = jax.random.randint(key_two, (devices, pair_count), PEER_SLOTS * load_level // 8, PEER_SLOTS * load_level // 4 + 1)
    chosen = jax.random.randint(key_three, (devices, 1), 0, pair_count)
    counts = jnp.where(jnp.arange(pair_count)[None, :] == chosen, PEER_SLOTS, counts)
    return counts.reshape(N_DOM, N_SUB * pair_count).astype(jnp.int32)


def draw_partner(key, part):
    devices = N_DOM * N_SUB
    faces = 6 * E_DEV
    device_keys = jax.random.split(jax.random.fold_in(key, 37), devices)

    def one_device(device_key):
        key_one, key_two = jax.random.split(device_key, 2)
        shuffle = jax.random.permutation(key_one, faces)
        values = jnp.concatenate([faces + jnp.arange(SOURCES), jax.random.randint(key_two, (faces - SOURCES,), 0, faces)])
        return values[jnp.argsort(shuffle)]
    partner_table = jax.vmap(one_device)(device_keys)
    return partner_table.reshape(N_DOM, N_SUB * faces).astype(jnp.int32)


def place_ends(result, rng, smallest, high):
    extent = result.shape
    spot = [jax.random.randint(jax.random.fold_in(rng, axis), (), 0, extent[axis]) for axis in range(len(extent))]
    result = result.at[tuple(spot)].set(smallest)
    longest = extent.index(max(extent))
    spot[longest] = (spot[longest] + 1) % extent[longest]
    return result.at[tuple(spot)].set(high)


def steps_of(key, shape, cuts, smallest, largest):
    factor_of = 1.0
    for axis_at, shards_of in cuts:
        draws = jax.random.uniform(jax.random.fold_in(jax.random.fold_in(key, 6), axis_at), (shards_of,), jnp.float32, smallest / len(cuts), largest / len(cuts))
        factor_of = factor_of * jnp.repeat(jnp.exp(draws), shape[axis_at] // shards_of).reshape((-1,) + (1,) * (len(shape) - 1 - axis_at))
    return factor_of


def noise(stream_key, shape, deviation, most, cuts=(), held_as=jnp.bfloat16):
    result = deviation * jax.random.normal(stream_key, shape, jnp.float32)
    if cuts:
        result = result * steps_of(stream_key, shape, cuts, -0.22, 0.18)
    return jnp.clip(result, -most, most).astype(held_as)


def setup_inputs(seed: int = 0) -> dict:
    splits = jax.random.split(jax.random.key(seed), 14)
    initial_state = noise(splits[0], (ROWS, ELEMS), 1.0, 6.0, ((1, 256),), jnp.float32)
    cotangent = noise(splits[1], (ROWS, ELEMS), 1.0, 6.0, ((1, 256),), jnp.float32)
    volume_operator = noise(splits[2], (ROWS, ROWS), ROWS ** -0.5, 0.3125)
    in_weight = noise(splits[3], (HIDDEN_SIZE, 2 * VARS), (2 * VARS) ** -0.5, 2.0)
    in_bias = noise(splits[4], (HIDDEN_SIZE,), 0.5, 3.0, (), jnp.float32)
    mid_weight = noise(splits[5], (HIDDEN_SIZE, HIDDEN_SIZE), HIDDEN_SIZE ** -0.5, 0.75)
    mid_bias = noise(splits[6], (HIDDEN_SIZE,), 0.5, 3.0, (), jnp.float32)
    out_weight = noise(splits[7], (VARS, HIDDEN_SIZE), HIDDEN_SIZE ** -0.5, 0.75)
    flux_matrix = noise(splits[8], (VARS, VARS), VARS ** -0.5, 2.5, (), jnp.float32)
    dom_send = place_ends(jax.random.randint(splits[9], (N_DOM, N_SUB * 2 * REACH * PEER_SLOTS), 0, 6 * E_DEV), jax.random.fold_in(splits[9], 1), 0, (6 * E_DEV) - 1).astype(jnp.int32)
    dom_count = draw_dom_count(jax.random.fold_in(splits[13], 71), 0)
    sub_send = place_ends(jax.random.randint(splits[11], (N_DOM, N_SUB * N_SUB * SUB_SLOTS), 0, 6 * E_DEV), jax.random.fold_in(splits[11], 1), 0, (6 * E_DEV) - 1).astype(jnp.int32)
    partner = draw_partner(jax.random.fold_in(splits[13], 71), 0)
    return dict(initial_state=initial_state, cotangent=cotangent, volume_operator=volume_operator, in_weight=in_weight, in_bias=in_bias, mid_weight=mid_weight, mid_bias=mid_bias, out_weight=out_weight, flux_matrix=flux_matrix, dom_send=dom_send, dom_count=dom_count, sub_send=sub_send, partner=partner)


time_step = 0.4
lift_gain = 1.5


def face_traces(values):
    elements = values.shape[-1]
    element_cube = values.reshape(5, 4, 4, 4, elements)
    face_blocks = [element_cube[:, :, :, 0, :], element_cube[:, :, :, 3, :], element_cube[:, :, 0, :, :], element_cube[:, :, 3, :, :], element_cube[:, 0, :, :, :], element_cube[:, 3, :, :, :]]
    stacked = jnp.stack([face_block.reshape(5, 16, elements) for face_block in face_blocks], axis=2)
    return stacked.reshape(80, 6 * elements)


def lift_traces(faces):
    elements = faces.shape[-1] // 6
    pieces = faces.reshape(5, 4, 4, 6, elements)
    element_cube = jnp.zeros((5, 4, 4, 4, elements), faces.dtype)
    element_cube = element_cube.at[:, :, :, 0, :].add(pieces[:, :, :, 0, :])
    element_cube = element_cube.at[:, :, :, 3, :].add(pieces[:, :, :, 1, :])
    element_cube = element_cube.at[:, :, 0, :, :].add(pieces[:, :, :, 2, :])
    element_cube = element_cube.at[:, :, 3, :, :].add(pieces[:, :, :, 3, :])
    element_cube = element_cube.at[:, 0, :, :, :].add(pieces[:, :, :, 4, :])
    element_cube = element_cube.at[:, 3, :, :, :].add(pieces[:, :, :, 5, :])
    return element_cube.reshape(320, elements)


def node_groups(values):
    elements = values.shape[-1]
    return jnp.moveaxis(values.reshape(values.shape[0] // 64, 8, 8 * elements), 1, 0)


def ungroup(blocks):
    return jnp.moveaxis(blocks, 0, 1).reshape(blocks.shape[1] * 64, blocks.shape[2] // 8)


def closure_net(field_b, volume_b, weights):
    in_weight, in_bias, mid_weight, mid_bias, out_weight = weights

    def one_block(members):
        inputs = jnp.concatenate(members, axis=0)
        first_act = jnp.tanh(jnp.dot(in_weight, inputs, preferred_element_type=jnp.float32) + in_bias[:, None]).astype(jnp.bfloat16)
        second_act = jnp.tanh(jnp.dot(mid_weight, first_act, preferred_element_type=jnp.float32) + mid_bias[:, None]).astype(jnp.bfloat16)
        return jnp.dot(out_weight, second_act, preferred_element_type=jnp.float32)

    return ungroup(lax.map(one_block, (node_groups(field_b), node_groups(volume_b))))


def closure_back(field_b, volume_b, upstream, weights):
    in_weight, in_bias, mid_weight, mid_bias, out_weight = weights

    def one_block(members):
        field_part, volume_part, upstream_part = members
        inputs = jnp.concatenate([field_part, volume_part], axis=0)
        first_act = jnp.tanh(jnp.dot(in_weight, inputs, preferred_element_type=jnp.float32) + in_bias[:, None])
        second_act = jnp.tanh(jnp.dot(mid_weight, first_act.astype(jnp.bfloat16), preferred_element_type=jnp.float32) + mid_bias[:, None])
        second_delta = (jnp.dot(out_weight.T, upstream_part.astype(jnp.bfloat16), preferred_element_type=jnp.float32) * (1.0 - second_act * second_act)).astype(jnp.bfloat16)
        first_delta = (jnp.dot(mid_weight.T, second_delta, preferred_element_type=jnp.float32) * (1.0 - first_act * first_act)).astype(jnp.bfloat16)
        return jnp.dot(in_weight.T, first_delta, preferred_element_type=jnp.float32)

    backward = ungroup(lax.map(one_block, (node_groups(field_b), node_groups(volume_b), node_groups(upstream))))
    return backward[:320], backward[320:]


def volume_terms(values, volume_operator, weights):
    field_b = values.astype(jnp.bfloat16)
    volume = jnp.dot(volume_operator, field_b, preferred_element_type=jnp.float32)
    closure = closure_net(field_b, volume.astype(jnp.bfloat16), weights)
    return volume + closure, face_traces(field_b)


def face_flux(traces, neighbours, flux_matrix):
    jump = neighbours.astype(jnp.float32) - traces.astype(jnp.float32)
    flux = jnp.dot(flux_matrix, jump.reshape(5, -1), precision=lax.Precision.HIGHEST).reshape(80, -1)
    return lift_gain * lift_traces(flux)


def faces_adjoint(adjoint, face_links, flux_matrix, source_total):
    face_grad = lift_gain * face_traces(adjoint)
    jump_grad = jnp.dot(flux_matrix.T, face_grad.reshape(5, -1), precision=lax.Precision.HIGHEST).reshape(80, -1)
    source_grad = jnp.zeros((80, source_total), jnp.float32).at[:, face_links].add(jump_grad)
    return jump_grad, source_grad


def rest_adjoint(values, adjoint, jump_grad, local_grad, dom_returned, sub_returned, dom_lists, sub_lists, volume_operator, weights):
    field_b = values.astype(jnp.bfloat16)
    volume_b = jnp.dot(volume_operator, field_b, preferred_element_type=jnp.float32).astype(jnp.bfloat16)
    trace_grad = (local_grad - jump_grad).at[:, dom_lists].add(dom_returned).at[:, sub_lists].add(sub_returned)
    field_grad, volume_grad = closure_back(field_b, volume_b, adjoint, weights)
    volume_total = (adjoint + volume_grad).astype(jnp.bfloat16)
    return jnp.dot(volume_operator.T, volume_total, preferred_element_type=jnp.float32) + field_grad + lift_traces(trace_grad)


def take_columns(table, columns):
    return jnp.take(table, columns, axis=1)


def reference(initial_state, cotangent, volume_operator, in_weight, in_bias, mid_weight, mid_bias, out_weight, flux_matrix, dom_send, dom_count, sub_send, partner):
    devices = N_DOM * N_SUB
    elements = E_DEV
    pair_count = 2 * REACH
    offsets = jnp.array(np.array([offset for offset in range(-REACH, REACH + 1) if offset != 0], dtype=np.int32))
    weights = (in_weight, in_bias, mid_weight, mid_bias, out_weight)
    dom_lists = dom_send.reshape(devices, pair_count * PEER_SLOTS)
    dom_mask = jnp.arange(PEER_SLOTS, dtype=jnp.int32)[None, None, :] < dom_count.reshape(devices, pair_count)[:, :, None]
    sub_lists = sub_send.reshape(devices, N_SUB * SUB_SLOTS)
    face_links = partner.reshape(devices, 6 * elements)
    source_total = 6 * elements + pair_count * PEER_SLOTS + N_SUB * SUB_SLOTS

    def split_rows(values):
        return values.reshape(320, devices, elements).transpose(1, 0, 2)

    def join_rows(values):
        return values.transpose(1, 0, 2).reshape(320, devices * elements)

    def route_dom(values, direction):
        layout = values.reshape(N_DOM, N_SUB, 80, pair_count, PEER_SLOTS)
        anchor = jnp.arange(N_DOM, dtype=jnp.int32)[:, None] - direction * offsets[None, :]
        inside = (anchor >= 0) & (anchor < N_DOM)
        picked = layout[jnp.clip(anchor, 0, N_DOM - 1), :, :, jnp.arange(pair_count, dtype=jnp.int32)[None, :], :]
        picked = jnp.where(inside[:, :, None, None, None], picked, jnp.zeros_like(picked))
        return picked.transpose(0, 2, 3, 1, 4).reshape(devices, 80, pair_count, PEER_SLOTS)

    def route_sub(values):
        layout = values.reshape(N_DOM, N_SUB, 80, N_SUB, SUB_SLOTS)
        return layout.transpose(0, 3, 2, 1, 4).reshape(devices, 80, N_SUB, SUB_SLOTS)

    def residual(fields):
        def local_front(values):
            return volume_terms(values, volume_operator, weights)

        base, traces = lax.map(local_front, fields)
        dom_sent = jax.vmap(take_columns)(traces, dom_lists).reshape(devices, 80, pair_count, PEER_SLOTS)
        dom_sent = jnp.where(dom_mask[:, None], dom_sent, jnp.zeros_like(dom_sent))
        sub_sent = jax.vmap(take_columns)(traces, sub_lists).reshape(devices, 80, N_SUB, SUB_SLOTS)
        dom_received = route_dom(dom_sent, 1).reshape(devices, 80, -1)
        sub_received = route_sub(sub_sent).reshape(devices, 80, -1)

        def local_back(members):
            base_part, trace_part, dom_part, sub_part, link_part = members
            sources = jnp.concatenate([trace_part, dom_part, sub_part], axis=1)
            return base_part + face_flux(trace_part, jnp.take(sources, link_part, axis=1), flux_matrix)

        return lax.map(local_back, (base, traces, dom_received, sub_received, face_links))

    def adjoint_of(fields, adjoints):
        def local_faces(members):
            return faces_adjoint(members[0], members[1], flux_matrix, source_total)

        jump_grad, source_grad = lax.map(local_faces, (adjoints, face_links))
        local_grad = source_grad[:, :, :6 * elements]
        dom_grad = source_grad[:, :, 6 * elements:6 * elements + pair_count * PEER_SLOTS].reshape(devices, 80, pair_count, PEER_SLOTS)
        sub_grad = source_grad[:, :, 6 * elements + pair_count * PEER_SLOTS:].reshape(devices, 80, N_SUB, SUB_SLOTS)
        dom_back = route_dom(dom_grad, -1)
        dom_returned = jnp.where(dom_mask[:, None], dom_back, jnp.zeros_like(dom_back)).reshape(devices, 80, -1)
        sub_returned = route_sub(sub_grad).reshape(devices, 80, -1)

        def local_rest(members):
            values, adjoint, jump_part, local_part, dom_part, sub_part, dom_part_lists, sub_part_lists = members
            return rest_adjoint(values, adjoint, jump_part, local_part, dom_part, sub_part, dom_part_lists, sub_part_lists, volume_operator, weights)

        return lax.map(local_rest, (fields, adjoints, jump_grad, local_grad, dom_returned, sub_returned, dom_lists, sub_lists))

    start_field = split_rows(initial_state)
    middle_field = start_field + time_step * residual(start_field)
    final_field = 0.5 * start_field + 0.5 * (middle_field + time_step * residual(middle_field))
    adjoint_final = split_rows(cotangent)
    adjoint_middle = 0.5 * adjoint_final + 0.5 * time_step * adjoint_of(middle_field, adjoint_final)
    adjoint_start = 0.5 * adjoint_final + adjoint_middle + time_step * adjoint_of(start_field, adjoint_middle)
    return join_rows(final_field), join_rows(adjoint_start)
```

```python
import jax
import jax.numpy as jnp
import numpy as np
from jax import lax
from jax.experimental import pallas as pl
from jax.experimental.pallas import tpu as pltpu
from jax.sharding import PartitionSpec as P

E = 256
LOCAL = 6 * E
OFFSETS = (-4, -3, -2, -1, 1, 2, 3, 4)
N_DOM = 64
STEP = 0.4
GAIN = 1.5
F32, BF16, I32 = jnp.float32, jnp.bfloat16, jnp.int32

SENT = (-2, None, 4, 1, -1, 2, -4, None, None, -3, None, 3)
ARRIVED = (-1, 2, 4, 3, -2, -3, -4, 1)


def block_of(offset):
    return OFFSETS.index(offset)


def face_nodes():
    nodes = np.zeros((6, 16), np.int32)
    for k in range(16):
        hi, lo = divmod(k, 4)
        nodes[:, k] = (4 * lo + 16 * hi, 3 + 4 * lo + 16 * hi, lo + 16 * hi, 12 + lo + 16 * hi, k, 48 + k)
    return nodes


def face_select():
    nodes = face_nodes()
    select = np.zeros((480, 320), np.float32)
    for f in range(6):
        for v in range(5):
            for k in range(16):
                select[f * 80 + v * 16 + k, v * 64 + nodes[f, k]] = 1.0
    return select


def dot(a, b):
    return lax.dot_general(a, b, (((1,), (0,)), ((), ())), preferred_element_type=F32)


def dot_t(a, b):
    return lax.dot_general(a, b, (((1,), (1,)), ((), ())), preferred_element_type=F32)


def iota(shape, dim):
    return lax.broadcasted_iota(I32, shape, dim)


def as_one(mask):
    return jnp.where(mask, 1.0, 0.0)


def split(x):
    hi = x.astype(BF16)
    return hi, (x - hi.astype(F32)).astype(BF16)


def one_hot(column, row):
    width = row.shape[1]
    parts = [as_one(column == row[:, i : i + 128]) for i in range(0, width, 128)]
    return jnp.concatenate(parts, axis=1).astype(BF16)


def by_group(index, groups, value_of):
    group = index // 32
    result = jnp.full(index.shape, -1, I32)
    for i, offset in enumerate(groups):
        if offset is not None:
            result = jnp.where(group == i, value_of(offset), result)
    return result


def in_range(offset, place, value):
    source = place - offset
    return jnp.where((source >= 0) & (source < N_DOM), value, -1)


def send_labels(dom_send, dom_count, groups, value_of):
    width = 32 * len(groups)
    slots = iota((8, E), 1)
    spread = as_one(iota((8, E), 0) == slots // 32).astype(BF16)
    counts = dot(jnp.broadcast_to(dom_count.astype(F32), (8, 8)).astype(BF16), spread)
    live = as_one((slots % 32).astype(F32) < counts)
    lists = jnp.broadcast_to(dom_send, (8, E))
    row = iota((8, E), 0)
    table = jnp.where(row == 0, (lists // 256).astype(F32), jnp.where(row == 1, (lists % 256).astype(F32), 1.0))
    table = (table * live).astype(BF16)
    lanes = iota((8, width), 1)
    source = by_group(lanes, groups, value_of)
    source = jnp.where(source >= 0, source * 32 + lanes % 32, -1)
    pick = as_one(iota((E, width), 0) == source[0:1, :]).astype(BF16)
    found = dot(table, pick)
    label = jnp.where(found[2:3] > 0.5, found[0:1] * 256.0 + found[1:2], -1.0)
    return label.astype(I32)


def recv_column(groups, start, rows, value_of):
    index = iota((rows, 128), 0) + start
    block = by_group(index, groups, value_of)
    return jnp.where(block >= 0, LOCAL + 32 * block + index % 32, -1)


def payload(field_b, g_hi, select_ref, partner, dom_send, dom_count, sub_send, outs):
    up_ref, down_ref, keep_ref, sub_ref = outs
    traces = dot(select_ref[...], field_b).astype(BF16)
    owed = dot(select_ref[...], g_hi).astype(BF16)
    owed = jnp.concatenate([owed[80 * f : 80 * f + 80] for f in range(6)], axis=1)
    labels = send_labels(dom_send, dom_count, SENT, block_of)
    labels = jnp.concatenate([labels, sub_send], axis=1)
    sent = jnp.zeros((80, 896), F32)
    for f in range(6):
        sent = sent + dot(traces[80 * f : 80 * f + 80], one_hot(iota((E, 128), 0) + f * E, labels))
    sent = sent.astype(BF16)
    back = dot_t(owed, one_hot(recv_column(SENT, 0, 384, lambda o: block_of(-o)), partner)).astype(BF16)
    for i, ref in enumerate((up_ref, down_ref, keep_ref)):
        ref[0:80, :] = sent[:, 128 * i : 128 * i + 128]
        ref[80:160, :] = back[:, 128 * i : 128 * i + 128]
    for half in range(2):
        column = iota((E, 128), 0) + (LOCAL + E + E * half)
        back = dot_t(owed, one_hot(column, partner)).astype(BF16)
        for i in range(2):
            t = 2 * half + i
            sub_ref[t, 0:80, :] = sent[:, 384 + 128 * t : 512 + 128 * t]
            sub_ref[t, 80:160, :] = back[:, 128 * i : 128 * i + 128]


def lifted(faces, lift_hi, lift_lo):
    hi, lo = split(faces)
    return dot(lift_hi, hi) + dot(lift_hi, lo) + dot(lift_lo, hi)


def stacked(rows):
    return jnp.concatenate([rows[:, E * f : E * f + E] for f in range(6)], axis=0)


def arrived_parts(place, first, second, sub_ref, partner, dom_send, dom_count, sub_send):
    def here(offset):
        return in_range(offset, place, block_of(offset))

    def mirrored(offset):
        return in_range(offset, place, block_of(-offset))

    arrived = jnp.concatenate([first[0:80], second[0:80]], axis=1)
    nbr = dot(arrived, one_hot(recv_column(ARRIVED, 0, E, here), partner))
    for half in range(2):
        column = iota((E, 128), 0) + (LOCAL + E + E * half)
        arrived = jnp.concatenate([sub_ref[2 * half, 0:80, :], sub_ref[2 * half + 1, 0:80, :]], axis=1)
        nbr = nbr + dot(arrived, one_hot(column, partner))
    labels = send_labels(dom_send, dom_count, ARRIVED, mirrored)
    labels = jnp.concatenate([labels, sub_send], axis=1)
    returned = jnp.concatenate(
        [first[80:160], second[80:160]] + [sub_ref[t, 80:160, :] for t in range(4)], axis=1
    )
    back = [dot_t(returned, one_hot(iota((E, 128), 0) + f * E, labels)) for f in range(6)]
    return stacked(nbr), jnp.concatenate(back, axis=0)


def local_parts(field_b, g, select_ref, partner):
    select = select_ref[...]
    traces = dot(select, field_b)
    g_hi, g_lo = split(g)
    owed_hi, owed_lo = dot(select, g_hi), dot(select, g_lo)
    pair = jnp.concatenate(
        [jnp.concatenate([owed_hi[80 * f : 80 * f + 80], owed_lo[80 * f : 80 * f + 80]], axis=0) for f in range(6)],
        axis=1,
    ).astype(BF16)
    traces_b = traces.astype(BF16)
    nbr = jnp.zeros((80, LOCAL), F32)
    back = []
    for f in range(6):
        pick = one_hot(iota((E, 128), 0) + f * E, partner)
        nbr = nbr + dot(traces_b[80 * f : 80 * f + 80], pick)
        both = dot_t(pair, pick)
        back.append(both[0:80] + both[80:160])
    return stacked(nbr) - traces, jnp.concatenate(back, axis=0) - (owed_hi + owed_lo)


def build_weights(in_weight, mid_weight, out_weight, flux, outs):
    a1, a1t, wm, wmt, a3, a3t, lift_hi, lift_lo, back_hi, back_lo = outs

    def mask(shape, condition, dtype=BF16):
        return as_one(condition(iota(shape, 0), iota(shape, 1))).astype(dtype)

    spread = mask((256, 64), lambda r, c: r // 4 == c)
    spread_t = mask((64, 256), lambda r, c: c // 4 == r)
    same = mask((256, 256), lambda r, c: r % 4 == c % 4, F32)
    wm[...] = (dot(dot(spread, mid_weight).astype(BF16), spread_t) * same).astype(BF16)
    wmt[...] = (dot(dot_t(spread, mid_weight).astype(BF16), spread_t) * same).astype(BF16)
    ten = mask((10, 160), lambda r, c: c // 16 == r)
    ten_t = mask((160, 10), lambda r, c: r // 16 == c)
    five = mask((5, 80), lambda r, c: c // 16 == r)
    five_t = mask((80, 5), lambda r, c: r // 16 == c)
    rows_in = dot(dot(spread, in_weight).astype(BF16), ten)
    cols_in = dot(dot_t(ten_t, in_weight).astype(BF16), spread_t)
    cols_out = dot(dot(five_t, out_weight).astype(BF16), spread_t)
    rows_out = dot(dot_t(spread, out_weight).astype(BF16), five)
    for s in range(4):
        a1[256 * s : 256 * s + 256, :] = (
            rows_in * mask((256, 160), lambda r, c: c % 16 == 4 * s + r % 4, F32)
        ).astype(BF16)
        a1t[:, 256 * s : 256 * s + 256] = (
            cols_in * mask((160, 256), lambda r, c: r % 16 == 4 * s + c % 4, F32)
        ).astype(BF16)
        a3[:, 256 * s : 256 * s + 256] = (
            cols_out * mask((80, 256), lambda r, c: r % 16 == 4 * s + c % 4, F32)
        ).astype(BF16)
        a3t[256 * s : 256 * s + 256, :] = (
            rows_out * mask((256, 80), lambda r, c: c % 16 == 4 * s + r % 4, F32)
        ).astype(BF16)
    lane = iota((8, 480), 1)
    f, k = lane // 80, lane % 16
    hi, lo = k // 4, k % 4
    node = jnp.where(f < 2, 4 * lo + 16 * hi + 3 * f, jnp.where(f < 4, lo + 16 * hi + 12 * (f - 2), k + 48 * (f - 4)))
    meets = as_one(iota((320, 480), 0) % 64 == node[0:1])
    var = mask((320, 5), lambda r, c: r // 64 == c)
    var_t = mask((5, 480), lambda r, c: (c % 80) // 16 == r)
    for part, forward, backward in zip(split(GAIN * flux), (lift_hi, lift_lo), (back_hi, back_lo)):
        forward[...] = (dot(dot(var, part).astype(BF16), var_t) * meets).astype(BF16)
        backward[...] = (dot(dot_t(var, part).astype(BF16), var_t) * meets).astype(BF16)


def wide(bias):
    return jnp.concatenate([bias, bias], axis=1)


def group_inputs(field_ref, volume_ref, start):
    rows = [field_ref[pl.ds(64 * v + start, 16), :] for v in range(5)]
    rows += [volume_ref[pl.ds(64 * v + start, 16), :] for v in range(5)]
    return jnp.concatenate(rows, axis=0)


def group_forward(inputs, a1, wm, bias_ref, s):
    h1 = jnp.tanh(dot(a1[256 * s : 256 * s + 256, :], inputs) + wide(bias_ref[0]))
    h2 = jnp.tanh(dot(wm[...], h1.astype(BF16)) + wide(bias_ref[1]))
    return h1, h2


def first_kernel(init_ref, cot_ref, select_ref, partner_ref, dom_send_ref, dom_count_ref, sub_send_ref, *outs):
    payload(
        init_ref[...].astype(BF16), cot_ref[...].astype(BF16), select_ref, partner_ref[...],
        dom_send_ref[...], dom_count_ref[...], sub_send_ref[...], outs,
    )


def second_kernel(
    init_ref, cot_ref, select_ref, partner_ref, volume_op_ref, in_ref, mid_ref, out_ref, flux_ref, bias_ref,
    part_ref, adj_ref, slope1_ref, slope2_ref, a1, a1t, wm, wmt, a3, a3t, lift_hi, lift_lo, back_hi, back_lo,
    field_s, volume_s,
):
    build_weights(
        in_ref[...], mid_ref[...], out_ref[...], flux_ref[...],
        (a1, a1t, wm, wmt, a3, a3t, lift_hi, lift_lo, back_hi, back_lo),
    )
    field_b = init_ref[...].astype(BF16)
    jump, trace_grad = local_parts(field_b, cot_ref[...], select_ref, partner_ref[...])
    adj_ref[...] = 0.5 * cot_ref[...] + (0.5 * STEP) * lifted(trace_grad, back_hi[...], back_lo[...])
    volume = dot(volume_op_ref[...], field_b)
    part_ref[...] = init_ref[...] + STEP * (volume + lifted(jump, lift_hi[...], lift_lo[...]))
    field_s[...] = field_b
    volume_s[...] = volume.astype(BF16)

    def group(i, carry):
        start = pl.multiple_of(16 * i, 16)
        inputs = group_inputs(field_s, volume_s, start)
        out = jnp.zeros((80, E), F32)
        for s in range(4):
            h1, h2 = group_forward(inputs, a1, wm, bias_ref, s)
            slope1_ref[i, 256 * s : 256 * s + 256, :] = (1.0 - h1 * h1).astype(BF16)
            slope2_ref[i, 256 * s : 256 * s + 256, :] = (1.0 - h2 * h2).astype(BF16)
            out = out + dot(a3[:, 256 * s : 256 * s + 256], h2.astype(BF16))
        for v in range(5):
            rows = pl.ds(64 * v + start, 16)
            part_ref[rows, :] = part_ref[rows, :] + STEP * out[16 * v : 16 * v + 16]
        return carry

    lax.fori_loop(0, 4, group, 0)


def third_kernel(
    place_ref, first_ref, second_ref, sub_ref, part_ref, adj_part_ref, cot_ref, select_ref, partner_ref,
    dom_send_ref, dom_count_ref, sub_send_ref, volume_op_ref, volume_op_t_ref, bias_ref,
    a1, a1t, wm, wmt, a3, a3t, lift_hi, lift_lo, back_hi, back_lo,
    middle_ref, base_ref, adj_ref, up_ref, down_ref, keep_ref, sub_out_ref,
    field_s, volume_s, cot_s, fgrad_s, vgrad_s,
):
    partner, dom_send, dom_count, sub_send = partner_ref[...], dom_send_ref[...], dom_count_ref[...], sub_send_ref[...]
    nbr, back = arrived_parts(
        place_ref[0], first_ref[...], second_ref[...], sub_ref, partner, dom_send, dom_count, sub_send
    )
    nbr_b = nbr.astype(BF16)
    middle = part_ref[...] + STEP * (dot(lift_hi[...], nbr_b) + dot(lift_lo[...], nbr_b))
    middle_ref[...] = middle
    adj_ref[...] = adj_part_ref[...] + (0.5 * STEP) * lifted(back, back_hi[...], back_lo[...])
    field_b = middle.astype(BF16)
    volume = dot(volume_op_ref[...], field_b)
    base_ref[...] = volume
    field_s[...] = field_b
    volume_s[...] = volume.astype(BF16)
    cot_s[...] = cot_ref[...].astype(BF16)

    def group(i, carry):
        start = pl.multiple_of(16 * i, 16)
        inputs = group_inputs(field_s, volume_s, start)
        upstream = jnp.concatenate([cot_s[pl.ds(64 * v + start, 16), :] for v in range(5)], axis=0)
        out = jnp.zeros((80, E), F32)
        grad = jnp.zeros((160, E), F32)
        for s in range(4):
            h1, h2 = group_forward(inputs, a1, wm, bias_ref, s)
            out = out + dot(a3[:, 256 * s : 256 * s + 256], h2.astype(BF16))
            delta = (dot(a3t[256 * s : 256 * s + 256, :], upstream) * (1.0 - h2 * h2)).astype(BF16)
            delta = (dot(wmt[...], delta) * (1.0 - h1 * h1)).astype(BF16)
            grad = grad + dot(a1t[:, 256 * s : 256 * s + 256], delta)
        for v in range(5):
            rows = pl.ds(64 * v + start, 16)
            base_ref[rows, :] = base_ref[rows, :] + out[16 * v : 16 * v + 16]
            fgrad_s[rows, :] = grad[16 * v : 16 * v + 16]
            vgrad_s[rows, :] = grad[80 + 16 * v : 96 + 16 * v]
        return carry

    lax.fori_loop(0, 4, group, 0)
    total = (cot_ref[...] + vgrad_s[...]).astype(BF16)
    adj = adj_ref[...] + (0.5 * STEP) * (dot(volume_op_t_ref[...], total) + fgrad_s[...])
    adj_ref[...] = adj
    payload(
        field_b, adj.astype(BF16), select_ref, partner, dom_send, dom_count, sub_send,
        (up_ref, down_ref, keep_ref, sub_out_ref),
    )


def fourth_kernel(
    init_ref, cot_ref, middle_ref, base_ref, adj_ref, select_ref, partner_ref, volume_op_t_ref,
    slope1_ref, slope2_ref, a1t, wmt, a3t, lift_hi, lift_lo, back_hi, back_lo,
    fin_ref, out_ref, adj_s, fgrad_s, vgrad_s,
):
    middle, adj = middle_ref[...], adj_ref[...]
    jump, trace_grad = local_parts(middle.astype(BF16), adj, select_ref, partner_ref[...])
    residual = base_ref[...] + lifted(jump, lift_hi[...], lift_lo[...])
    fin_ref[...] = 0.5 * init_ref[...] + 0.5 * (middle + STEP * residual)
    adj_s[...] = adj.astype(BF16)

    def group(i, carry):
        start = pl.multiple_of(16 * i, 16)
        upstream = jnp.concatenate([adj_s[pl.ds(64 * v + start, 16), :] for v in range(5)], axis=0)
        grad = jnp.zeros((160, E), F32)
        for s in range(4):
            rows = slice(256 * s, 256 * s + 256)
            delta = (dot(a3t[rows, :], upstream) * slope2_ref[i, rows, :].astype(F32)).astype(BF16)
            delta = (dot(wmt[...], delta) * slope1_ref[i, rows, :].astype(F32)).astype(BF16)
            grad = grad + dot(a1t[:, rows], delta)
        for v in range(5):
            rows = pl.ds(64 * v + start, 16)
            fgrad_s[rows, :] = grad[16 * v : 16 * v + 16]
            vgrad_s[rows, :] = grad[80 + 16 * v : 96 + 16 * v]
        return carry

    lax.fori_loop(0, 4, group, 0)
    total = (adj + vgrad_s[...]).astype(BF16)
    local = dot(volume_op_t_ref[...], total) + fgrad_s[...] + lifted(trace_grad, back_hi[...], back_lo[...])
    out_ref[...] = 0.5 * cot_ref[...] + adj + STEP * local


def fifth_kernel(
    place_ref, first_ref, second_ref, sub_ref, fin_part_ref, out_part_ref, partner_ref,
    dom_send_ref, dom_count_ref, sub_send_ref, lift_hi, lift_lo, back_hi, back_lo, fin_ref, out_ref,
):
    nbr, back = arrived_parts(
        place_ref[0], first_ref[...], second_ref[...], sub_ref, partner_ref[...],
        dom_send_ref[...], dom_count_ref[...], sub_send_ref[...],
    )
    nbr_b = nbr.astype(BF16)
    fin_ref[...] = fin_part_ref[...] + (0.5 * STEP) * (dot(lift_hi[...], nbr_b) + dot(lift_lo[...], nbr_b))
    out_ref[...] = out_part_ref[...] + STEP * lifted(back, back_hi[...], back_lo[...])


def call(kernel, name, outs, inputs, scratch=(), scalars=0, cost=None):
    specs = [pl.BlockSpec(memory_space=pltpu.SMEM)] * scalars
    specs += [pl.BlockSpec(memory_space=pltpu.VMEM)] * (len(inputs) - scalars)
    return pl.pallas_call(
        kernel,
        name=name,
        out_shape=[jax.ShapeDtypeStruct(shape, dtype) for shape, dtype in outs],
        in_specs=specs,
        out_specs=[pl.BlockSpec(memory_space=pltpu.VMEM)] * len(outs),
        scratch_shapes=[pltpu.VMEM(shape, dtype) for shape, dtype in scratch],
        cost_estimate=cost,
    )(*inputs)


PAYLOAD = [((160, 128), BF16)] * 3 + [((4, 160, 128), BF16)]
STATE = ((320, E), F32)
STATE_B = ((320, E), BF16)
MATRICES = [
    ((1024, 160), BF16), ((160, 1024), BF16), ((256, 256), BF16), ((256, 256), BF16),
    ((80, 1024), BF16), ((1024, 80), BF16),
    ((320, 480), BF16), ((320, 480), BF16), ((320, 480), BF16), ((320, 480), BF16),
]
COST = pl.CostEstimate(flops=10_000_000_000, transcendentals=0, bytes_accessed=8_000_000)


def exchange(up, down, keep, sub):
    def around(x, distance):
        return lax.ppermute(x, "dom", [(i, (i + distance) % N_DOM) for i in range(N_DOM)])

    group = iota((160, 128), 1) // 32
    sub = lax.all_to_all(sub, "sub", 0, 0, tiled=True)
    up, down = around(up, 1), around(down, -1)
    far_up = around(jnp.where(group == 1, down, jnp.where(group == 2, up, keep)), 3)
    far_down = around(jnp.where(group == 0, up, jnp.where(group == 2, down, keep)), -3)
    first = jnp.where(group == 0, down, far_up)
    second = jnp.where(group == 3, up, far_down)
    return first, second, sub


def body(
    initial_state, cotangent, volume_operator, in_weight, in_bias, mid_weight, mid_bias, out_weight, flux_matrix,
    dom_send, dom_count, sub_send, partner,
):
    select = jnp.asarray(face_select(), BF16)
    place = lax.axis_index("dom").astype(I32).reshape(1)
    volume_t = volume_operator.T
    bias = jnp.broadcast_to(jnp.repeat(jnp.stack([in_bias, mid_bias]), 4, axis=1)[:, :, None], (2, 256, 128))
    lists = (partner, dom_send, dom_count, sub_send)

    sent = call(first_kernel, "first", PAYLOAD, (initial_state, cotangent, select) + lists)
    arrived = exchange(*sent)
    part, adj_part, slope1, slope2, *mats = call(
        second_kernel, "second",
        [STATE, STATE, ((4, 1024, E), BF16), ((4, 1024, E), BF16)] + MATRICES,
        (initial_state, cotangent, select, partner, volume_operator, in_weight, mid_weight, out_weight, flux_matrix, bias),
        [STATE_B, STATE_B], cost=COST,
    )
    a1, a1t, wm, wmt, a3, a3t, *lifts = mats
    middle, base, adj, *sent = call(
        third_kernel, "third", [STATE, STATE, STATE] + PAYLOAD,
        (place, *arrived, part, adj_part, cotangent, select, *lists, volume_operator, volume_t, bias, *mats),
        [STATE_B, STATE_B, STATE_B, STATE, STATE], scalars=1,
    )
    arrived = exchange(*sent)
    fin_part, out_part = call(
        fourth_kernel, "fourth", [STATE, STATE],
        (initial_state, cotangent, middle, base, adj, select, partner, volume_t, slope1, slope2, a1t, wmt, a3t, *lifts),
        [STATE_B, STATE, STATE], cost=COST,
    )
    final_state, adjoint_state = call(
        fifth_kernel, "fifth", [STATE, STATE],
        (place, *arrived, fin_part, out_part, *lists, *lifts), scalars=1,
    )
    return final_state, adjoint_state


def solution(mesh):
    columns = P(None, ("dom", "sub"))
    pairs = P("dom", "sub")
    return jax.shard_map(
        body,
        mesh=mesh,
        in_specs=(columns, columns, P(), P(), P(), P(), P(), P(), P(), pairs, pairs, pairs, pairs),
        out_specs=(columns, columns),
        check_vma=False,
    )
```

```python
import jax
import jax.numpy as jnp
import numpy as np
from jax import lax
from jax.experimental import pallas as pl
from jax.experimental.pallas import tpu as pltpu
from jax.sharding import PartitionSpec as P

E = 256
LOCAL = 6 * E
OFFSETS = (-4, -3, -2, -1, 1, 2, 3, 4)
N_DOM = 64
STEP = 0.4
GAIN = 1.5
F32, BF16, I32 = jnp.float32, jnp.bfloat16, jnp.int32

SENT = (
    (2, 3, -2, -1, None, 4, -3, -4, 1, None, None, None),
    (2, 1, -2, -3, 3, 4, None, -4, None, None, -1, None),
)
ARRIVED = (
    (2, 4, -2, -4, 3, 1, -1, -3),
    (2, 4, -2, -4, 1, 3, -3, -1),
)


def block_of(offset):
    return OFFSETS.index(offset)


def face_nodes():
    nodes = np.zeros((6, 16), np.int32)
    for k in range(16):
        hi, lo = divmod(k, 4)
        nodes[:, k] = (4 * lo + 16 * hi, 3 + 4 * lo + 16 * hi, lo + 16 * hi, 12 + lo + 16 * hi, k, 48 + k)
    return nodes


def face_select():
    nodes = face_nodes()
    select = np.zeros((480, 320), np.float32)
    for f in range(6):
        for v in range(5):
            for k in range(16):
                select[f * 80 + v * 16 + k, v * 64 + nodes[f, k]] = 1.0
    return select


def dot(a, b):
    return lax.dot_general(a, b, (((1,), (0,)), ((), ())), preferred_element_type=F32)


def dot_t(a, b):
    return lax.dot_general(a, b, (((1,), (1,)), ((), ())), preferred_element_type=F32)


def dot_first(a, b):
    return lax.dot_general(a, b, (((0,), (0,)), ((), ())), preferred_element_type=F32)


def iota(shape, dim):
    return lax.broadcasted_iota(I32, shape, dim)


def as_one(mask):
    return jnp.where(mask, 1.0, 0.0)


def split(x):
    hi = x.astype(BF16)
    return hi, (x - hi.astype(F32)).astype(BF16)


def pick_group(index, core, groups, value_of):
    group = index // 32
    result = jnp.full(index.shape, -1, I32)
    for i, pair in enumerate(zip(*groups)):
        low, high = [-1 if offset is None else value_of(offset) for offset in pair]
        if low >= 0 or high >= 0:
            result = jnp.where(group == i, low if low == high else jnp.where(core == 0, low, high), result)
    return result


def dom_labels(dom_send, dom_count, core, groups, value_of):
    width = 32 * len(groups[0])
    slots = iota((8, E), 1)
    spread = as_one(iota((8, E), 0) == slots // 32).astype(BF16)
    counts = dot(jnp.broadcast_to(dom_count.astype(F32), (8, 8)).astype(BF16), spread)
    live = as_one((slots % 32).astype(F32) < counts)
    lists = jnp.broadcast_to(dom_send, (8, E))
    row = iota((8, E), 0)
    table = jnp.where(row == 0, (lists // 256).astype(F32), jnp.where(row == 1, (lists % 256).astype(F32), 1.0))
    table = (table * live).astype(BF16)
    lanes = iota((8, width), 1)
    source = pick_group(lanes, core, groups, value_of)
    source = jnp.where(source >= 0, source * 32 + lanes % 32, -1)
    pick = as_one(iota((E, width), 0) == source[0:1, :]).astype(BF16)
    found = dot(table, pick)
    label = jnp.where(found[2:3] > 0.5, found[0:1] * 256.0 + found[1:2], -1.0)
    return label.astype(I32)


def sub_labels(sub_send, sub):
    blocks = [sub_send[:, 128 * t : 128 * t + 128] for t in range(4)]
    result = []
    for k in range(4):
        block = blocks[k]
        for s in range(1, 4):
            block = jnp.where(sub == s, blocks[s ^ k], block)
        result.append(block)
    return result


def source_rows(partner, core, sub, groups, value_of, width):
    received = partner - LOCAL
    block = received >> 5
    place = jnp.full(partner.shape, -1, I32)
    for j in range(8):
        spots = []
        for side in groups:
            spots.append([i for i, offset in enumerate(side) if offset is not None and value_of(offset) == j][0])
        low, high = spots
        place = jnp.where(block == j, 32 * (low if low == high else jnp.where(core == 0, low, high)), place)
    place = place + (received & 31)
    over = received - E
    over = width + (((over >> 7) ^ sub) << 7) + (over & 127)
    return jnp.where(received >= E, over, jnp.where(received >= 0, place, -1))


def low_hot(row):
    column = iota((E, 128), 0)
    parts = [as_one(column == (row[:, i : i + 128] & 255)) for i in range(0, row.shape[1], 128)]
    return jnp.concatenate(parts, axis=1).astype(BF16)


def gather(blocks, row, count):
    rows = blocks.shape[0] // count
    out = []
    for start in range(0, row.shape[1], 256):
        part = row[:, start : start + 256]
        found = dot(blocks, low_hot(part))
        taken = jnp.zeros((rows, part.shape[1]), F32)
        for b in range(count):
            taken = jnp.where(part >> 8 == b, found[rows * b : rows * b + rows], taken)
        out.append(taken)
    return out


def scatter(values, row, count):
    block = row >> 8
    spread = [values * as_one(block == b).astype(BF16) for b in range(count)]
    return dot_t(jnp.concatenate(spread, axis=0), low_hot(row))


def payload(field_b, g_hi, select_ref, partner, dom_send, dom_count, sub_send, core, sub, outs):
    traces = dot(select_ref[...], field_b).astype(BF16)
    owed = dot(select_ref[...], g_hi).astype(BF16)
    owed = jnp.concatenate([owed[80 * f : 80 * f + 80] for f in range(6)], axis=1)
    labels = dom_labels(dom_send, dom_count, core, SENT, block_of)
    labels = jnp.concatenate([labels] + sub_labels(sub_send, sub), axis=1)
    sent = jnp.concatenate(gather(traces, labels, 6), axis=1).astype(BF16)
    places = source_rows(partner, core, sub, SENT, lambda o: block_of(-o), 384)
    back = scatter(owed, places, 4).astype(BF16)
    for i, ref in enumerate(outs):
        ref[0:80, :] = sent[:, 128 * i : 128 * i + 128]
        b, half = divmod(i, 2)
        ref[80:160, :] = back[80 * b : 80 * b + 80, 128 * half : 128 * half + 128]


def lifted(faces, lift_hi, lift_lo):
    hi, lo = split(faces)
    return dot(lift_hi, hi) + dot(lift_hi, lo) + dot(lift_lo, hi)


def arrived_parts(arrays, partner, dom_send, dom_count, sub_send, core, sub):
    plus_two, minus_two, plus_four, minus_four, other = [ref[...] for ref in arrays[:5]]
    group = iota((160, 128), 1) // 32
    direct = jnp.where(group == 0, plus_two, jnp.where(group == 1, plus_four, jnp.where(group == 2, minus_two, minus_four)))
    parts = [direct, other] + [ref[...] for ref in arrays[5:]]
    traces = [jnp.concatenate([parts[2 * b][0:80], parts[2 * b + 1][0:80]], axis=1) for b in range(3)]
    places = source_rows(partner, core, sub, ARRIVED, block_of, 256)
    nbr = jnp.concatenate(gather(jnp.concatenate(traces, axis=0), places, 3), axis=0)
    labels = dom_labels(dom_send, dom_count, core, ARRIVED, lambda o: block_of(-o))
    labels = jnp.concatenate([labels] + sub_labels(sub_send, sub), axis=1)
    returned = jnp.concatenate([part[80:160] for part in parts], axis=1)
    return nbr, scatter(returned, labels, 6)


def local_parts(field_b, g, select_ref, partner):
    select = select_ref[...]
    traces = dot(select, field_b)
    g_hi, g_lo = split(g)
    owed_hi, owed_lo = dot(select, g_hi), dot(select, g_lo)
    pair = jnp.concatenate(
        [jnp.concatenate([owed_hi[80 * f : 80 * f + 80], owed_lo[80 * f : 80 * f + 80]], axis=0) for f in range(6)],
        axis=1,
    ).astype(BF16)
    nbr = jnp.concatenate(gather(traces.astype(BF16), partner, 6), axis=0)
    back = scatter(pair, partner, 6)
    back = jnp.concatenate([back[160 * f : 160 * f + 80] + back[160 * f + 80 : 160 * f + 160] for f in range(6)], axis=0)
    return nbr - traces, back - (owed_hi + owed_lo)


def build_weights(in_t, mid_weight, out_weight, flux, biases, outs):
    a1, a1t, wm, wmt, a3, a3t, lift_hi, lift_lo, back_hi, back_lo, bias_ref = outs

    def mask(shape, condition, dtype=BF16):
        return as_one(condition(iota(shape, 0), iota(shape, 1))).astype(dtype)

    spread = mask((256, 64), lambda r, c: r // 4 == c)
    spread_t = mask((64, 256), lambda r, c: c // 4 == r)
    same = mask((256, 256), lambda r, c: r % 4 == c % 4, F32)
    wm[...] = (dot(dot(spread, mid_weight).astype(BF16), spread_t) * same).astype(BF16)
    wmt[...] = (dot(dot_t(spread, mid_weight).astype(BF16), spread_t) * same).astype(BF16)
    ten = mask((10, 160), lambda r, c: c // 16 == r)
    ten_t = mask((160, 10), lambda r, c: r // 16 == c)
    five = mask((5, 80), lambda r, c: c // 16 == r)
    five_t = mask((80, 5), lambda r, c: r // 16 == c)
    rows_in = dot(dot_t(spread, in_t).astype(BF16), ten)
    cols_in = dot(dot(ten_t, in_t).astype(BF16), spread_t)
    cols_out = dot(dot(five_t, out_weight).astype(BF16), spread_t)
    rows_out = dot(dot_t(spread, out_weight).astype(BF16), five)
    for s in range(4):
        a1[256 * s : 256 * s + 256, :] = (
            rows_in * mask((256, 160), lambda r, c: c % 16 == 4 * s + r % 4, F32)
        ).astype(BF16)
        a1t[:, 256 * s : 256 * s + 256] = (
            cols_in * mask((160, 256), lambda r, c: r % 16 == 4 * s + c % 4, F32)
        ).astype(BF16)
        a3[:, 256 * s : 256 * s + 256] = (
            cols_out * mask((80, 256), lambda r, c: r % 16 == 4 * s + c % 4, F32)
        ).astype(BF16)
        a3t[256 * s : 256 * s + 256, :] = (
            rows_out * mask((256, 80), lambda r, c: c % 16 == 4 * s + r % 4, F32)
        ).astype(BF16)
    ones = jnp.ones((64, 128), BF16)
    for i, bias in enumerate(biases):
        hi, rest = split(bias)
        mid, low = split(bias - hi.astype(F32))
        bias_ref[i] = dot(spread * hi, ones) + dot(spread * mid, ones) + dot(spread * low, ones)
    lane = iota((8, 480), 1)
    f, k = lane // 80, lane % 16
    hi, lo = k // 4, k % 4
    node = jnp.where(f < 2, 4 * lo + 16 * hi + 3 * f, jnp.where(f < 4, lo + 16 * hi + 12 * (f - 2), k + 48 * (f - 4)))
    meets = as_one(iota((320, 480), 0) % 64 == node[0:1])
    var = mask((320, 5), lambda r, c: r // 64 == c)
    var_t = mask((5, 480), lambda r, c: (c % 80) // 16 == r)
    for part, forward, backward in zip(split(GAIN * flux), (lift_hi, lift_lo), (back_hi, back_lo)):
        forward[...] = (dot(dot(var, part).astype(BF16), var_t) * meets).astype(BF16)
        backward[...] = (dot(dot_t(var, part).astype(BF16), var_t) * meets).astype(BF16)


def wide(bias):
    return jnp.concatenate([bias, bias], axis=1)


def quarter(s):
    return slice(256 * s, 256 * s + 256)


def group_rows(ref, start):
    return jnp.concatenate([ref[pl.ds(64 * v + start, 16), :] for v in range(5)], axis=0)


def group_inputs(field_ref, volume_ref, start):
    return jnp.concatenate([group_rows(field_ref, start), group_rows(volume_ref, start)], axis=0)


def first_kernel(place_ref, init_ref, cot_ref, select_ref, partner_ref, dom_send_ref, dom_count_ref, sub_send_ref, *outs):
    payload(
        init_ref[...].astype(BF16), cot_ref[...].astype(BF16), select_ref, partner_ref[...],
        dom_send_ref[...], dom_count_ref[...], sub_send_ref[...], place_ref[0], place_ref[1], outs,
    )


def second_kernel(
    init_ref, cot_ref, select_ref, partner_ref, volume_op_ref, in_ref, mid_ref, out_ref, flux_ref,
    in_bias_ref, mid_bias_ref,
    part_ref, adj_ref, slope1_ref, slope2_ref, a1, a1t, wm, wmt, a3, a3t, lift_hi, lift_lo, back_hi, back_lo, bias_ref,
    field_s, volume_s, h_s,
):
    build_weights(
        in_ref[...], mid_ref[...], out_ref[...], flux_ref[...], (in_bias_ref[...], mid_bias_ref[...]),
        (a1, a1t, wm, wmt, a3, a3t, lift_hi, lift_lo, back_hi, back_lo, bias_ref),
    )
    field_b = init_ref[...].astype(BF16)
    jump, trace_grad = local_parts(field_b, cot_ref[...], select_ref, partner_ref[...])
    adj_ref[...] = 0.5 * cot_ref[...] + (0.5 * STEP) * lifted(trace_grad, back_hi[...], back_lo[...])
    volume = dot(volume_op_ref[...], field_b)
    part_ref[...] = init_ref[...] + STEP * (volume + lifted(jump, lift_hi[...], lift_lo[...]))
    field_s[...] = field_b
    volume_s[...] = volume.astype(BF16)

    def group(i, carry):
        start = pl.multiple_of(16 * i, 16)
        inputs = group_inputs(field_s, volume_s, start)
        for s in range(4):
            h1 = jnp.tanh(dot(a1[quarter(s), :], inputs) + wide(bias_ref[0]))
            h_s[0, quarter(s), :] = h1.astype(BF16)
            slope1_ref[i, quarter(s), :] = (1.0 - h1 * h1).astype(BF16)
        for s in range(4):
            h2 = jnp.tanh(dot(wm[...], h_s[0, quarter(s), :]) + wide(bias_ref[1]))
            h_s[1, quarter(s), :] = h2.astype(BF16)
            slope2_ref[i, quarter(s), :] = (1.0 - h2 * h2).astype(BF16)
        out = dot(a3[...], h_s[1])
        for v in range(5):
            rows = pl.ds(64 * v + start, 16)
            part_ref[rows, :] = part_ref[rows, :] + STEP * out[16 * v : 16 * v + 16]
        return carry

    lax.fori_loop(0, 4, group, 0)


def third_kernel(
    place_ref, *refs,
):
    arrays, refs = refs[:9], refs[9:]
    (
        part_ref, adj_part_ref, cot_ref, select_ref, partner_ref,
        dom_send_ref, dom_count_ref, sub_send_ref, volume_op_ref,
        a1, a1t, wm, wmt, a3, a3t, lift_hi, lift_lo, back_hi, back_lo, bias_ref,
        middle_ref, base_ref, adj_ref, *sent_refs,
    ) = refs[:30]
    field_s, volume_s, cot_s, fgrad_s, vgrad_s, h_s, slope_s, delta_s = refs[30:]
    core, sub = place_ref[0], place_ref[1]
    partner, dom_send, dom_count, sub_send = partner_ref[...], dom_send_ref[...], dom_count_ref[...], sub_send_ref[...]
    nbr, back = arrived_parts(arrays, partner, dom_send, dom_count, sub_send, core, sub)
    nbr_b = nbr.astype(BF16)
    middle = part_ref[...] + STEP * (dot(lift_hi[...], nbr_b) + dot(lift_lo[...], nbr_b))
    middle_ref[...] = middle
    adj_ref[...] = adj_part_ref[...] + (0.5 * STEP) * lifted(back, back_hi[...], back_lo[...])
    field_b = middle.astype(BF16)
    volume = dot(volume_op_ref[...], field_b)
    base_ref[...] = volume
    field_s[...] = field_b
    volume_s[...] = volume.astype(BF16)
    cot_s[...] = cot_ref[...].astype(BF16)

    def group(i, carry):
        start = pl.multiple_of(16 * i, 16)
        inputs = group_inputs(field_s, volume_s, start)
        upstream = group_rows(cot_s, start)
        for s in range(4):
            h1 = jnp.tanh(dot(a1[quarter(s), :], inputs) + wide(bias_ref[0]))
            h_s[0, quarter(s), :] = h1.astype(BF16)
            slope_s[quarter(s), :] = 1.0 - h1 * h1
        for s in range(4):
            h2 = jnp.tanh(dot(wm[...], h_s[0, quarter(s), :]) + wide(bias_ref[1]))
            h_s[1, quarter(s), :] = h2.astype(BF16)
            delta_s[0, quarter(s), :] = (dot(a3t[quarter(s), :], upstream) * (1.0 - h2 * h2)).astype(BF16)
        out = dot(a3[...], h_s[1])
        for s in range(4):
            delta_s[1, quarter(s), :] = (dot(wmt[...], delta_s[0, quarter(s), :]) * slope_s[quarter(s), :]).astype(BF16)
        grad = dot(a1t[...], delta_s[1])
        for v in range(5):
            rows = pl.ds(64 * v + start, 16)
            base_ref[rows, :] = base_ref[rows, :] + out[16 * v : 16 * v + 16]
            fgrad_s[rows, :] = grad[16 * v : 16 * v + 16]
            vgrad_s[rows, :] = grad[80 + 16 * v : 96 + 16 * v]
        return carry

    lax.fori_loop(0, 4, group, 0)
    total = (cot_ref[...] + vgrad_s[...]).astype(BF16)
    adj = adj_ref[...] + (0.5 * STEP) * (dot_first(volume_op_ref[...], total) + fgrad_s[...])
    adj_ref[...] = adj
    payload(field_b, adj.astype(BF16), select_ref, partner, dom_send, dom_count, sub_send, core, sub, sent_refs)


def fourth_kernel(
    init_ref, cot_ref, middle_ref, base_ref, adj_ref, select_ref, partner_ref, volume_op_ref,
    slope1_ref, slope2_ref, a1t, wmt, a3t, lift_hi, lift_lo, back_hi, back_lo,
    fin_ref, out_ref, adj_s, fgrad_s, vgrad_s, delta_s,
):
    middle, adj = middle_ref[...], adj_ref[...]
    jump, trace_grad = local_parts(middle.astype(BF16), adj, select_ref, partner_ref[...])
    residual = base_ref[...] + lifted(jump, lift_hi[...], lift_lo[...])
    fin_ref[...] = 0.5 * init_ref[...] + 0.5 * (middle + STEP * residual)
    out_ref[...] = lifted(trace_grad, back_hi[...], back_lo[...])
    adj_s[...] = adj.astype(BF16)

    def group(i, carry):
        start = pl.multiple_of(16 * i, 16)
        upstream = group_rows(adj_s, start)
        for s in range(4):
            delta = dot(a3t[quarter(s), :], upstream) * slope2_ref[i, quarter(s), :].astype(F32)
            delta_s[0, quarter(s), :] = delta.astype(BF16)
        for s in range(4):
            delta = dot(wmt[...], delta_s[0, quarter(s), :]) * slope1_ref[i, quarter(s), :].astype(F32)
            delta_s[1, quarter(s), :] = delta.astype(BF16)
        grad = dot(a1t[...], delta_s[1])
        for v in range(5):
            rows = pl.ds(64 * v + start, 16)
            fgrad_s[rows, :] = grad[16 * v : 16 * v + 16]
            vgrad_s[rows, :] = grad[80 + 16 * v : 96 + 16 * v]
        return carry

    lax.fori_loop(0, 4, group, 0)
    adj = adj_ref[...]
    total = (adj + vgrad_s[...]).astype(BF16)
    local = dot_first(volume_op_ref[...], total) + fgrad_s[...] + out_ref[...]
    out_ref[...] = 0.5 * cot_ref[...] + adj + STEP * local


def fifth_kernel(place_ref, *refs):
    arrays, refs = refs[:9], refs[9:]
    (
        fin_part_ref, out_part_ref, partner_ref, dom_send_ref, dom_count_ref, sub_send_ref,
        lift_hi, lift_lo, back_hi, back_lo, fin_ref, out_ref,
    ) = refs
    nbr, back = arrived_parts(
        arrays, partner_ref[...], dom_send_ref[...], dom_count_ref[...], sub_send_ref[...], place_ref[0], place_ref[1]
    )
    nbr_b = nbr.astype(BF16)
    fin_ref[...] = fin_part_ref[...] + (0.5 * STEP) * (dot(lift_hi[...], nbr_b) + dot(lift_lo[...], nbr_b))
    out_ref[...] = out_part_ref[...] + STEP * lifted(back, back_hi[...], back_lo[...])


def call(kernel, name, outs, inputs, scratch=(), scalars=0, cost=None, final=False):
    specs = [pl.BlockSpec(memory_space=pltpu.SMEM)] * scalars
    specs += [pl.BlockSpec(memory_space=pltpu.VMEM)] * (len(inputs) - scalars)
    kind = jax.ShapeDtypeStruct if final else pltpu.VMEM
    return pl.pallas_call(
        kernel,
        name=name,
        out_shape=[kind(shape, dtype) for shape, dtype in outs],
        in_specs=specs,
        out_specs=[pl.BlockSpec(memory_space=pltpu.VMEM)] * len(outs),
        scratch_shapes=[pltpu.VMEM(shape, dtype) for shape, dtype in scratch],
        cost_estimate=cost,
        compiler_params=pltpu.CompilerParams(vmem_limit_bytes=30 * 1024 * 1024),
    )(*inputs)


PAYLOAD = [((160, 128), BF16)] * 7
STATE = ((320, E), F32)
STATE_B = ((320, E), BF16)
MATRICES = [
    ((1024, 160), BF16), ((160, 1024), BF16), ((256, 256), BF16), ((256, 256), BF16),
    ((80, 1024), BF16), ((1024, 80), BF16),
    ((320, 480), BF16), ((320, 480), BF16), ((320, 480), BF16), ((320, 480), BF16), ((2, 256, 128), F32),
]
PAIR = ((2, 1024, E), BF16)
COST = pl.CostEstimate(flops=10_000_000_000, transcendentals=0, bytes_accessed=8_000_000)


def exchange(near, far, own, sub_own, *sub_sent):
    def along(x, distance):
        devices = range(N_DOM)
        return lax.ppermute(x, "dom", [(i, i + distance) for i in devices if i + distance in devices])

    plus_four, minus_four = along(far, 4), along(far, -4)
    plus_two, minus_two = along(near, 2), along(near, -2)
    subs = [lax.ppermute(x, "sub", [(i, i ^ k) for i in range(4)]) for k, x in zip((1, 2, 3), sub_sent)]
    group = iota((160, 128), 1) // 32
    other = jnp.where(group == 0, plus_four, jnp.where(group == 1, plus_two, jnp.where(group == 2, minus_four, minus_two)))
    other = jnp.where(group % 2 == 0, other + own, other)
    other = lax.ppermute(other, "dom", [(i, i ^ 1) for i in range(N_DOM)])
    return plus_two, minus_two, plus_four, minus_four, other, sub_own, *subs


def body(
    initial_state, cotangent, volume_operator, in_weight, in_bias, mid_weight, mid_bias, out_weight, flux_matrix,
    dom_send, dom_count, sub_send, partner,
):
    select = jnp.asarray(face_select(), BF16)
    place = jnp.stack([lax.axis_index("dom") % 2, lax.axis_index("sub")]).astype(I32)
    lists = (partner, dom_send, dom_count, sub_send)

    sent = call(first_kernel, "first", PAYLOAD, (place, initial_state, cotangent, select) + lists, scalars=1)
    arrived = exchange(*sent)
    part, adj_part, slope1, slope2, *mats = call(
        second_kernel, "second",
        [STATE, STATE, ((4, 1024, E), BF16), ((4, 1024, E), BF16)] + MATRICES,
        (
            initial_state, cotangent, select, partner, volume_operator, in_weight.T, mid_weight, out_weight,
            flux_matrix, in_bias.reshape(1, 64), mid_bias.reshape(1, 64),
        ),
        [STATE_B, STATE_B, PAIR], cost=COST,
    )
    a1, a1t, wm, wmt, a3, a3t, *lifts, bias = mats
    middle, base, adj, *sent = call(
        third_kernel, "third", [STATE, STATE, STATE] + PAYLOAD,
        (place, *arrived, part, adj_part, cotangent, select, *lists, volume_operator, *mats),
        [STATE_B, STATE_B, STATE_B, STATE, STATE, PAIR, ((1024, E), F32), PAIR], scalars=1,
    )
    arrived = exchange(*sent)
    fin_part, out_part = call(
        fourth_kernel, "fourth", [STATE, STATE],
        (
            initial_state, cotangent, middle, base, adj, select, partner, volume_operator, slope1, slope2,
            a1t, wmt, a3t, *lifts,
        ),
        [STATE_B, STATE, STATE, PAIR], cost=COST,
    )
    final_state, adjoint_state = call(
        fifth_kernel, "fifth", [STATE, STATE],
        (place, *arrived, fin_part, out_part, *lists, *lifts), scalars=1, final=True,
    )
    return final_state, adjoint_state


def solution(mesh):
    columns = P(None, ("dom", "sub"))
    pairs = P("dom", "sub")
    return jax.shard_map(
        body,
        mesh=mesh,
        in_specs=(columns, columns, P(), P(), P(), P(), P(), P(), P(), pairs, pairs, pairs, pairs),
        out_specs=(columns, columns),
        check_vma=False,
    )
```

```python
import jax
import jax.numpy as jnp
import numpy as np
from jax import lax
from jax.experimental import pallas as pl
from jax.experimental.pallas import tpu as pltpu
from jax.sharding import PartitionSpec as P

E = 256
LOCAL = 6 * E
OFFSETS = (-4, -3, -2, -1, 1, 2, 3, 4)
N_DOM = 64
STEP = 0.4
GAIN = 1.5
F32, BF16, I32 = jnp.float32, jnp.bfloat16, jnp.int32


def block_of(offset):
    return OFFSETS.index(offset)


def to_core(d):
    return d ^ 1


def to_pair(d):
    return d ^ 2


def to_both(d):
    return d ^ 3


def reversed_even(d):
    return d ^ 6


def reversed_odd(d):
    chip, core = divmod(d, 2)
    other = ((chip + 2) ^ 3) - 2
    return 2 * other + core if 0 <= other < N_DOM // 2 else d


def takes_both(d):
    return (d % 2 == 0) == (d // 4 % 2 == 0)


def sent_offsets(d):
    chip, core = divmod(d, 2)
    side = 1 - 2 * (chip % 2)
    cross = 1 - 2 * core
    first = (2 * side, 4 * cross, -4 * cross, -2 * side)
    second = (cross - 2 * side, cross, -3 * cross, cross + 2 * side)
    return first + second


def routing_tables():
    hold = {d: [(d, o) for o in sent_offsets(d)] for d in range(N_DOM)}
    rows = []
    forward = {}
    for d in range(N_DOM):
        pair, core, both = hold[to_pair(d)][:4], hold[to_core(d)][4:], hold[to_both(d)][4:]
        even = [core[0], pair[1], both[2] if takes_both(d) else pair[2], hold[d][3]]
        odd = [core[0], pair[1], pair[2] if takes_both(d) else both[2], hold[d][3]]
        forward[d] = even, odd, [pair[0], core[1], None, both[3]]
    for d in range(N_DOM):
        found = forward[d][2] + forward[reversed_even(d)][0] + forward[reversed_odd(d)][1]
        arrived = [None] * 12
        for i, item in enumerate(found):
            if item is not None and item[0] != d and sum(item) == d and item[1] not in arrived:
                arrived[i] = item[1]
        wanted = [o for o in OFFSETS if 0 <= d - o < N_DOM]
        assert sorted(o for o in arrived if o is not None) == wanted
        sent = sent_offsets(d)
        assert sorted(sent) == list(OFFSETS)
        row = [block_of(o) for o in sent]
        row += [sent.index(-o) for o in OFFSETS]
        row += [-1 if o is None else block_of(-o) for o in arrived]
        row += [arrived.index(o) if o in arrived else -1 for o in OFFSETS]
        rows.append(row)
    return np.array(rows, np.int32)


SENT_BLOCK, SENT_PLACE, ARRIVED_BLOCK, ARRIVED_PLACE, TABLE_WIDTH = 0, 8, 16, 28, 36


def face_nodes():
    nodes = np.zeros((6, 16), np.int32)
    for k in range(16):
        hi, lo = divmod(k, 4)
        nodes[:, k] = (4 * lo + 16 * hi, 3 + 4 * lo + 16 * hi, lo + 16 * hi, 12 + lo + 16 * hi, k, 48 + k)
    return nodes


def face_select():
    nodes = face_nodes()
    select = np.zeros((480, 320), np.float32)
    for f in range(6):
        for v in range(5):
            for k in range(16):
                select[f * 80 + v * 16 + k, v * 64 + nodes[f, k]] = 1.0
    return select


def dot(a, b):
    return lax.dot_general(a, b, (((1,), (0,)), ((), ())), preferred_element_type=F32)


def dot_t(a, b):
    return lax.dot_general(a, b, (((1,), (1,)), ((), ())), preferred_element_type=F32)


def dot_first(a, b):
    return lax.dot_general(a, b, (((0,), (0,)), ((), ())), preferred_element_type=F32)


def iota(shape, dim):
    return lax.broadcasted_iota(I32, shape, dim)


def as_one(mask):
    return jnp.where(mask, 1.0, 0.0)


def split(x):
    hi = x.astype(BF16)
    return hi, (x - hi.astype(F32)).astype(BF16)


def dom_labels(dom_send, dom_count, blocks):
    width = 32 * len(blocks)
    slots = iota((8, E), 1)
    spread = as_one(iota((8, E), 0) == slots // 32).astype(BF16)
    counts = dot(jnp.broadcast_to(dom_count.astype(F32), (8, 8)).astype(BF16), spread)
    live = as_one((slots % 32).astype(F32) < counts)
    lists = jnp.broadcast_to(dom_send, (8, E))
    row = iota((8, E), 0)
    table = jnp.where(row == 0, (lists // 256).astype(F32), jnp.where(row == 1, (lists % 256).astype(F32), 1.0))
    table = (table * live).astype(BF16)
    lanes = iota((8, width), 1)
    source = jnp.full(lanes.shape, -1, I32)
    for i, block in enumerate(blocks):
        source = jnp.where(lanes >> 5 == i, block, source)
    source = jnp.where(source >= 0, source * 32 + (lanes & 31), -1)
    pick = as_one(iota((E, width), 0) == source[0:1, :]).astype(BF16)
    found = dot(table, pick)
    label = jnp.where(found[2:3] > 0.5, found[0:1] * 256.0 + found[1:2], -1.0)
    return label.astype(I32)


def sub_labels(sub_send, sub):
    blocks = [sub_send[:, 128 * t : 128 * t + 128] for t in range(4)]
    result = []
    for k in range(4):
        block = blocks[k]
        for s in range(1, 4):
            block = jnp.where(sub == s, blocks[s ^ k], block)
        result.append(block)
    return result


def source_rows(partner, sub, places, width):
    received = partner - LOCAL
    block = received >> 5
    place = jnp.full(partner.shape, -32, I32)
    for j, group in enumerate(places):
        place = jnp.where(block == j, 32 * group, place)
    place = place + (received & 31)
    over = received - E
    over = width + (((over >> 7) ^ sub) << 7) + (over & 127)
    return jnp.where(received >= E, over, jnp.where(received >= 0, place, -1))


def low_hot(row):
    column = iota((E, 128), 0)
    parts = [as_one(column == (row[:, i : i + 128] & 255)) for i in range(0, row.shape[1], 128)]
    return jnp.concatenate(parts, axis=1).astype(BF16)


def gather(blocks, row, count):
    rows = blocks.shape[0] // count
    out = []
    for start in range(0, row.shape[1], 256):
        part = row[:, start : start + 256]
        found = dot(blocks, low_hot(part))
        taken = jnp.zeros((rows, part.shape[1]), F32)
        for b in range(count):
            taken = jnp.where(part >> 8 == b, found[rows * b : rows * b + rows], taken)
        out.append(taken)
    return out


def scatter(values, row, count):
    block = row >> 8
    spread = [values * as_one(block == b).astype(BF16) for b in range(count)]
    return dot_t(jnp.concatenate(spread, axis=0), low_hot(row))


def payload(field_b, g_hi, select_ref, partner, dom_send, dom_count, sub_send, route, sub, outs):
    traces = dot(select_ref[...], field_b).astype(BF16)
    owed = dot(select_ref[...], g_hi).astype(BF16)
    owed = jnp.concatenate([owed[80 * f : 80 * f + 80] for f in range(6)], axis=1)
    labels = dom_labels(dom_send, dom_count, route(SENT_BLOCK, 8))
    labels = jnp.concatenate([labels] + sub_labels(sub_send, sub), axis=1)
    sent = jnp.concatenate(gather(traces, labels, 6), axis=1).astype(BF16)
    places = source_rows(partner, sub, route(SENT_PLACE, 8), E)
    back = scatter(owed, places, 3).astype(BF16)
    for i, ref in enumerate(outs):
        ref[0:80, :] = sent[:, 128 * i : 128 * i + 128]
        b, half = divmod(i, 2)
        ref[80:160, :] = back[80 * b : 80 * b + 80, 128 * half : 128 * half + 128]


def lifted(faces, lift_hi, lift_lo):
    hi, lo = split(faces)
    return dot(lift_hi, hi) + dot(lift_hi, lo) + dot(lift_lo, hi)


def arrived_parts(arrays, partner, dom_send, dom_count, sub_send, route, sub):
    pair, core, both, even, odd = [ref[...] for ref in arrays[:5]]
    group = iota((160, 128), 1) // 32
    direct = jnp.where(group == 0, pair, jnp.where(group == 1, core, both))
    parts = [direct, even, odd] + [ref[...] for ref in arrays[5:]]
    traces = [jnp.concatenate([parts[2 * b][0:80], parts[min(2 * b + 1, 6)][0:80]], axis=1) for b in range(4)]
    places = source_rows(partner, sub, route(ARRIVED_PLACE, 8), 384)
    nbr = jnp.concatenate(gather(jnp.concatenate(traces, axis=0), places, 4), axis=0)
    labels = dom_labels(dom_send, dom_count, route(ARRIVED_BLOCK, 12))
    labels = jnp.concatenate([labels] + sub_labels(sub_send, sub), axis=1)
    returned = jnp.concatenate([part[80:160] for part in parts], axis=1)
    return nbr, scatter(returned, labels, 6)


def local_parts(field_b, g, select_ref, partner):
    select = select_ref[...]
    traces = dot(select, field_b)
    g_hi, g_lo = split(g)
    owed_hi, owed_lo = dot(select, g_hi), dot(select, g_lo)
    pair = jnp.concatenate(
        [jnp.concatenate([owed_hi[80 * f : 80 * f + 80], owed_lo[80 * f : 80 * f + 80]], axis=0) for f in range(6)],
        axis=1,
    ).astype(BF16)
    nbr = jnp.concatenate(gather(traces.astype(BF16), partner, 6), axis=0)
    back = scatter(pair, partner, 6)
    back = jnp.concatenate([back[160 * f : 160 * f + 80] + back[160 * f + 80 : 160 * f + 160] for f in range(6)], axis=0)
    return nbr - traces, back - (owed_hi + owed_lo)


def build_weights(in_t, mid_weight, out_weight, flux, biases, outs):
    a1, a1t, wm, wmt, a3, a3t, lift_hi, lift_lo, back_hi, back_lo, bias_ref = outs

    def mask(shape, condition, dtype=BF16):
        return as_one(condition(iota(shape, 0), iota(shape, 1))).astype(dtype)

    spread = mask((256, 64), lambda r, c: r // 4 == c)
    spread_t = mask((64, 256), lambda r, c: c // 4 == r)
    same = mask((256, 256), lambda r, c: r % 4 == c % 4, F32)
    wm[...] = (dot(dot(spread, mid_weight).astype(BF16), spread_t) * same).astype(BF16)
    wmt[...] = (dot(dot_t(spread, mid_weight).astype(BF16), spread_t) * same).astype(BF16)
    ten = mask((10, 160), lambda r, c: c // 16 == r)
    ten_t = mask((160, 10), lambda r, c: r // 16 == c)
    five = mask((5, 80), lambda r, c: c // 16 == r)
    five_t = mask((80, 5), lambda r, c: r // 16 == c)
    rows_in = dot(dot_t(spread, in_t).astype(BF16), ten)
    cols_in = dot(dot(ten_t, in_t).astype(BF16), spread_t)
    cols_out = dot(dot(five_t, out_weight).astype(BF16), spread_t)
    rows_out = dot(dot_t(spread, out_weight).astype(BF16), five)
    for s in range(4):
        a1[256 * s : 256 * s + 256, :] = (
            rows_in * mask((256, 160), lambda r, c: c % 16 == 4 * s + r % 4, F32)
        ).astype(BF16)
        a1t[:, 256 * s : 256 * s + 256] = (
            cols_in * mask((160, 256), lambda r, c: r % 16 == 4 * s + c % 4, F32)
        ).astype(BF16)
        a3[:, 256 * s : 256 * s + 256] = (
            cols_out * mask((80, 256), lambda r, c: r % 16 == 4 * s + c % 4, F32)
        ).astype(BF16)
        a3t[256 * s : 256 * s + 256, :] = (
            rows_out * mask((256, 80), lambda r, c: c % 16 == 4 * s + r % 4, F32)
        ).astype(BF16)
    ones = jnp.ones((64, 128), BF16)
    for i, bias in enumerate(biases):
        hi, rest = split(bias)
        mid, low = split(bias - hi.astype(F32))
        bias_ref[i] = dot(spread * hi, ones) + dot(spread * mid, ones) + dot(spread * low, ones)
    lane = iota((8, 480), 1)
    f, k = lane // 80, lane % 16
    hi, lo = k // 4, k % 4
    node = jnp.where(f < 2, 4 * lo + 16 * hi + 3 * f, jnp.where(f < 4, lo + 16 * hi + 12 * (f - 2), k + 48 * (f - 4)))
    meets = as_one(iota((320, 480), 0) % 64 == node[0:1])
    var = mask((320, 5), lambda r, c: r // 64 == c)
    var_t = mask((5, 480), lambda r, c: (c % 80) // 16 == r)
    for part, forward, backward in zip(split(GAIN * flux), (lift_hi, lift_lo), (back_hi, back_lo)):
        forward[...] = (dot(dot(var, part).astype(BF16), var_t) * meets).astype(BF16)
        backward[...] = (dot(dot_t(var, part).astype(BF16), var_t) * meets).astype(BF16)


def wide(bias):
    return jnp.concatenate([bias, bias], axis=1)


def quarter(s):
    return slice(256 * s, 256 * s + 256)


def group_rows(ref, start):
    return jnp.concatenate([ref[pl.ds(64 * v + start, 16), :] for v in range(5)], axis=0)


def group_inputs(field_ref, volume_ref, start):
    return jnp.concatenate([group_rows(field_ref, start), group_rows(volume_ref, start)], axis=0)


def route_of(place_ref, table_ref):
    row = place_ref[0] * TABLE_WIDTH

    def route(start, count):
        return [table_ref[row + start + i] for i in range(count)]

    return route


def first_kernel(place_ref, table_ref, *refs):
    count = (len(refs) - 7) // 2
    sources, copies, sems = refs[:count], refs[count : 2 * count], refs[-1]
    outs = refs[2 * count : -1]
    moves = [pltpu.make_async_copy(a, b, sems.at[i]) for i, (a, b) in enumerate(zip(sources, copies))]
    for move in moves:
        move.start()
    for move in moves[:7]:
        move.wait()
    init_ref, cot_ref, select_ref, partner_ref, dom_send_ref, dom_count_ref, sub_send_ref = copies[:7]
    payload(
        init_ref[...].astype(BF16), cot_ref[...].astype(BF16), select_ref, partner_ref[...],
        dom_send_ref[...], dom_count_ref[...], sub_send_ref[...], route_of(place_ref, table_ref), place_ref[1], outs,
    )
    for move in moves[7:]:
        move.wait()


def second_kernel(
    init_ref, cot_ref, select_ref, partner_ref, volume_op_ref, in_ref, mid_ref, out_ref, flux_ref,
    in_bias_ref, mid_bias_ref,
    part_ref, adj_ref, slope1_ref, slope2_ref, a1, a1t, wm, wmt, a3, a3t, lift_hi, lift_lo, back_hi, back_lo, bias_ref,
    field_s, volume_s, h_s,
):
    build_weights(
        in_ref[...], mid_ref[...], out_ref[...], flux_ref[...], (in_bias_ref[...], mid_bias_ref[...]),
        (a1, a1t, wm, wmt, a3, a3t, lift_hi, lift_lo, back_hi, back_lo, bias_ref),
    )
    field_b = init_ref[...].astype(BF16)
    jump, trace_grad = local_parts(field_b, cot_ref[...], select_ref, partner_ref[...])
    adj_ref[...] = 0.5 * cot_ref[...] + (0.5 * STEP) * lifted(trace_grad, back_hi[...], back_lo[...])
    volume = dot(volume_op_ref[...], field_b)
    part_ref[...] = init_ref[...] + STEP * (volume + lifted(jump, lift_hi[...], lift_lo[...]))
    field_s[...] = field_b
    volume_s[...] = volume.astype(BF16)

    def group(i, carry):
        start = pl.multiple_of(16 * i, 16)
        inputs = group_inputs(field_s, volume_s, start)
        for s in range(4):
            h1 = jnp.tanh(dot(a1[quarter(s), :], inputs) + wide(bias_ref[0]))
            h_s[0, quarter(s), :] = h1.astype(BF16)
            slope1_ref[i, quarter(s), :] = (1.0 - h1 * h1).astype(BF16)
        for s in range(4):
            h2 = jnp.tanh(dot(wm[...], h_s[0, quarter(s), :]) + wide(bias_ref[1]))
            h_s[1, quarter(s), :] = h2.astype(BF16)
            slope2_ref[i, quarter(s), :] = (1.0 - h2 * h2).astype(BF16)
        out = dot(a3[...], h_s[1])
        for v in range(5):
            rows = pl.ds(64 * v + start, 16)
            part_ref[rows, :] = part_ref[rows, :] + STEP * out[16 * v : 16 * v + 16]
        return carry

    lax.fori_loop(0, 4, group, 0)


def third_kernel(place_ref, table_ref, *refs):
    arrays, refs = refs[:9], refs[9:]
    (
        part_ref, adj_part_ref, cot_ref, select_ref, partner_ref,
        dom_send_ref, dom_count_ref, sub_send_ref, volume_op_ref,
        a1, a1t, wm, wmt, a3, a3t, lift_hi, lift_lo, back_hi, back_lo, bias_ref,
        middle_ref, base_ref, adj_ref, *sent_refs,
    ) = refs[:29]
    field_s, volume_s, cot_s, fgrad_s, vgrad_s, h_s, slope_s, delta_s = refs[29:]
    route, sub = route_of(place_ref, table_ref), place_ref[1]
    partner, dom_send, dom_count, sub_send = partner_ref[...], dom_send_ref[...], dom_count_ref[...], sub_send_ref[...]
    nbr, back = arrived_parts(arrays, partner, dom_send, dom_count, sub_send, route, sub)
    nbr_b = nbr.astype(BF16)
    middle = part_ref[...] + STEP * (dot(lift_hi[...], nbr_b) + dot(lift_lo[...], nbr_b))
    middle_ref[...] = middle
    adj_ref[...] = adj_part_ref[...] + (0.5 * STEP) * lifted(back, back_hi[...], back_lo[...])
    field_b = middle.astype(BF16)
    volume = dot(volume_op_ref[...], field_b)
    base_ref[...] = volume
    field_s[...] = field_b
    volume_s[...] = volume.astype(BF16)
    cot_s[...] = cot_ref[...].astype(BF16)

    def group(i, carry):
        start = pl.multiple_of(16 * i, 16)
        inputs = group_inputs(field_s, volume_s, start)
        upstream = group_rows(cot_s, start)
        for s in range(4):
            h1 = jnp.tanh(dot(a1[quarter(s), :], inputs) + wide(bias_ref[0]))
            h_s[0, quarter(s), :] = h1.astype(BF16)
            slope_s[quarter(s), :] = 1.0 - h1 * h1
        for s in range(4):
            h2 = jnp.tanh(dot(wm[...], h_s[0, quarter(s), :]) + wide(bias_ref[1]))
            h_s[1, quarter(s), :] = h2.astype(BF16)
            delta_s[0, quarter(s), :] = (dot(a3t[quarter(s), :], upstream) * (1.0 - h2 * h2)).astype(BF16)
        out = dot(a3[...], h_s[1])
        for s in range(4):
            delta_s[1, quarter(s), :] = (dot(wmt[...], delta_s[0, quarter(s), :]) * slope_s[quarter(s), :]).astype(BF16)
        grad = dot(a1t[...], delta_s[1])
        for v in range(5):
            rows = pl.ds(64 * v + start, 16)
            base_ref[rows, :] = base_ref[rows, :] + out[16 * v : 16 * v + 16]
            fgrad_s[rows, :] = grad[16 * v : 16 * v + 16]
            vgrad_s[rows, :] = grad[80 + 16 * v : 96 + 16 * v]
        return carry

    lax.fori_loop(0, 4, group, 0)
    total = (cot_ref[...] + vgrad_s[...]).astype(BF16)
    adj = adj_ref[...] + (0.5 * STEP) * (dot_first(volume_op_ref[...], total) + fgrad_s[...])
    adj_ref[...] = adj
    payload(field_b, adj.astype(BF16), select_ref, partner, dom_send, dom_count, sub_send, route, sub, sent_refs)


def fourth_kernel(
    init_ref, cot_ref, middle_ref, base_ref, adj_ref, select_ref, partner_ref, volume_op_ref,
    slope1_ref, slope2_ref, a1t, wmt, a3t, lift_hi, lift_lo, back_hi, back_lo,
    fin_ref, out_ref, adj_s, fgrad_s, vgrad_s, delta_s,
):
    middle, adj = middle_ref[...], adj_ref[...]
    jump, trace_grad = local_parts(middle.astype(BF16), adj, select_ref, partner_ref[...])
    residual = base_ref[...] + lifted(jump, lift_hi[...], lift_lo[...])
    fin_ref[...] = 0.5 * init_ref[...] + 0.5 * (middle + STEP * residual)
    out_ref[...] = lifted(trace_grad, back_hi[...], back_lo[...])
    adj_s[...] = adj.astype(BF16)

    def group(i, carry):
        start = pl.multiple_of(16 * i, 16)
        upstream = group_rows(adj_s, start)
        for s in range(4):
            delta = dot(a3t[quarter(s), :], upstream) * slope2_ref[i, quarter(s), :].astype(F32)
            delta_s[0, quarter(s), :] = delta.astype(BF16)
        for s in range(4):
            delta = dot(wmt[...], delta_s[0, quarter(s), :]) * slope1_ref[i, quarter(s), :].astype(F32)
            delta_s[1, quarter(s), :] = delta.astype(BF16)
        grad = dot(a1t[...], delta_s[1])
        for v in range(5):
            rows = pl.ds(64 * v + start, 16)
            fgrad_s[rows, :] = grad[16 * v : 16 * v + 16]
            vgrad_s[rows, :] = grad[80 + 16 * v : 96 + 16 * v]
        return carry

    lax.fori_loop(0, 4, group, 0)
    adj = adj_ref[...]
    total = (adj + vgrad_s[...]).astype(BF16)
    local = dot_first(volume_op_ref[...], total) + fgrad_s[...] + out_ref[...]
    out_ref[...] = 0.5 * cot_ref[...] + adj + STEP * local


def fifth_kernel(place_ref, table_ref, *refs):
    arrays, refs = refs[:9], refs[9:]
    (
        fin_part_ref, out_part_ref, partner_ref, dom_send_ref, dom_count_ref, sub_send_ref,
        lift_hi, lift_lo, back_hi, back_lo, fin_ref, out_ref,
    ) = refs
    nbr, back = arrived_parts(
        arrays, partner_ref[...], dom_send_ref[...], dom_count_ref[...], sub_send_ref[...],
        route_of(place_ref, table_ref), place_ref[1],
    )
    nbr_b = nbr.astype(BF16)
    fin_ref[...] = fin_part_ref[...] + (0.5 * STEP) * (dot(lift_hi[...], nbr_b) + dot(lift_lo[...], nbr_b))
    out_ref[...] = out_part_ref[...] + STEP * lifted(back, back_hi[...], back_lo[...])


def call(kernel, name, outs, inputs, scratch=(), scalars=0, cost=None, final=False, raw=False):
    specs = [pl.BlockSpec(memory_space=pltpu.SMEM)] * scalars
    specs += [pl.BlockSpec(memory_space=pltpu.HBM if raw else pltpu.VMEM)] * (len(inputs) - scalars)
    kind = jax.ShapeDtypeStruct if final else pltpu.VMEM
    if scalars:
        inputs = (inputs[0], pltpu.with_memory_space_constraint(inputs[1], pltpu.HBM)) + tuple(inputs[2:])
    if raw:
        inputs = inputs[:scalars] + tuple(pltpu.with_memory_space_constraint(x, pltpu.HBM) for x in inputs[scalars:])
        scratch = [pltpu.SemaphoreType.DMA((len(inputs) - scalars,))]
    else:
        scratch = [pltpu.VMEM(shape, dtype) for shape, dtype in scratch]
    return pl.pallas_call(
        kernel,
        name=name,
        out_shape=[kind(shape, dtype) for shape, dtype in outs],
        in_specs=specs,
        out_specs=[pl.BlockSpec(memory_space=pltpu.VMEM)] * len(outs),
        scratch_shapes=scratch,
        cost_estimate=cost,
        compiler_params=pltpu.CompilerParams(vmem_limit_bytes=30 * 1024 * 1024),
    )(*inputs)


PAYLOAD = [((160, 128), BF16)] * 6
STATE = ((320, E), F32)
STATE_B = ((320, E), BF16)
MATRICES = [
    ((1024, 160), BF16), ((160, 1024), BF16), ((256, 256), BF16), ((256, 256), BF16),
    ((80, 1024), BF16), ((1024, 80), BF16),
    ((320, 480), BF16), ((320, 480), BF16), ((320, 480), BF16), ((320, 480), BF16), ((2, 256, 128), F32),
]
PAIR = ((2, 1024, E), BF16)
COST = pl.CostEstimate(flops=10_000_000_000, transcendentals=0, bytes_accessed=8_000_000)


def exchange(place, first, second, sub_own, *sub_sent):
    def hop(x, target):
        return lax.ppermute(x, "dom", [(d, target(d)) for d in range(N_DOM)])

    core, pair, both = hop(second, to_core), hop(first, to_pair), hop(second, to_both)
    subs = [lax.ppermute(x, "sub", [(i, i ^ k) for i in range(4)]) for k, x in zip((1, 2, 3), sub_sent)]
    group = iota((160, 128), 1) // 32
    taken = ((place[0] ^ (place[0] >> 2)) & 1) == 0
    edge = jnp.where(group == 0, core, jnp.where(group == 3, first, pair))
    even = jnp.where((group == 2) & taken, both, edge)
    odd = jnp.where((group == 2) & ~taken, both, edge)
    return pair, core, both, hop(even, reversed_even), hop(odd, reversed_odd), sub_own, *subs


def body(
    initial_state, cotangent, volume_operator, in_weight, in_bias, mid_weight, mid_bias, out_weight, flux_matrix,
    dom_send, dom_count, sub_send, partner,
):
    select = jnp.asarray(face_select(), BF16)
    table = jnp.asarray(routing_tables().reshape(-1))
    place = jnp.stack([lax.axis_index("dom"), lax.axis_index("sub")]).astype(I32)
    raw = (
        initial_state, cotangent, select, partner, dom_send, dom_count, sub_send,
        volume_operator, in_weight.T, mid_weight, out_weight, flux_matrix, in_bias.reshape(1, 64), mid_bias.reshape(1, 64),
    )
    copies = [(x.shape, x.dtype) for x in raw]
    done = call(first_kernel, "first", copies + PAYLOAD, (place, table) + raw, scalars=2, raw=True)
    initial_state, cotangent, select, partner, dom_send, dom_count, sub_send, volume_operator = done[:8]
    lists = (partner, dom_send, dom_count, sub_send)
    arrived = exchange(place, *done[len(raw):])
    part, adj_part, slope1, slope2, *mats = call(
        second_kernel, "second",
        [STATE, STATE, ((4, 1024, E), BF16), ((4, 1024, E), BF16)] + MATRICES,
        (initial_state, cotangent, select, partner, *done[7 : len(raw)]),
        [STATE_B, STATE_B, PAIR], cost=COST,
    )
    a1, a1t, wm, wmt, a3, a3t, *lifts, bias = mats
    middle, base, adj, *sent = call(
        third_kernel, "third", [STATE, STATE, STATE] + PAYLOAD,
        (place, table, *arrived, part, adj_part, cotangent, select, *lists, volume_operator, *mats),
        [STATE_B, STATE_B, STATE_B, STATE, STATE, PAIR, ((1024, E), F32), PAIR], scalars=2,
    )
    arrived = exchange(place, *sent)
    fin_part, out_part = call(
        fourth_kernel, "fourth", [STATE, STATE],
        (
            initial_state, cotangent, middle, base, adj, select, partner, volume_operator, slope1, slope2,
            a1t, wmt, a3t, *lifts,
        ),
        [STATE_B, STATE, STATE, PAIR], cost=COST,
    )
    final_state, adjoint_state = call(
        fifth_kernel, "fifth", [STATE, STATE],
        (place, table, *arrived, fin_part, out_part, *lists, *lifts), scalars=2, final=True,
    )
    return final_state, adjoint_state


def solution(mesh):
    columns = P(None, ("dom", "sub"))
    pairs = P("dom", "sub")
    return jax.shard_map(
        body,
        mesh=mesh,
        in_specs=(columns, columns, P(), P(), P(), P(), P(), P(), P(), pairs, pairs, pairs, pairs),
        out_specs=(columns, columns),
        check_vma=False,
    )
```

```python
import jax
import jax.numpy as jnp
import numpy as np
from jax import lax
from jax.experimental import pallas as pl
from jax.experimental.pallas import tpu as pltpu
from jax.sharding import PartitionSpec as P

E = 256
LOCAL = 6 * E
OFFSETS = (-4, -3, -2, -1, 1, 2, 3, 4)
N_DOM = 64
STEP = 0.4
GAIN = 1.5
F32, BF16, I32 = jnp.float32, jnp.bfloat16, jnp.int32


def block_of(offset):
    return OFFSETS.index(offset)


def to_core(d):
    return d ^ 1


def to_pair(d):
    return d ^ 2


def reversed_even(d):
    return d ^ 6


def reversed_odd(d):
    chip, core = divmod(d, 2)
    other = ((chip + 2) ^ 3) - 2
    return 2 * other + core if 0 <= other < N_DOM // 2 else d


def sent_offsets(d):
    return (2, -2, 4, -4) + ((-3, 1, -1, 3) if d % 2 else (-1, 3, -3, 1))


def routing_tables():
    hold = {d: [(d, o) for o in sent_offsets(d)] for d in range(N_DOM)}
    core = {d: hold[to_core(d)][4:] for d in range(N_DOM)}
    even, odd, direct = {}, {}, {}
    for d in range(N_DOM):
        same, other = hold[to_pair(d)][:4], core[to_pair(d)]
        up = [hold[d][0], core[d][1], same[2], other[3]]
        down = [core[d][0], hold[d][1], other[2], same[3]]
        even[d], odd[d] = (down, up) if d // 4 % 2 else (up, down)
        direct[d] = ([same[0], other[1]] if d // 2 % 2 else [other[0], same[1]]) + core[d][2:]
    rows = []
    for d in range(N_DOM):
        found = direct[d] + even[reversed_even(d)] + odd[reversed_odd(d)]
        arrived = [None] * 12
        for i, item in enumerate(found):
            if item[0] != d and sum(item) == d and item[1] not in arrived:
                arrived[i] = item[1]
        wanted = [o for o in OFFSETS if 0 <= d - o < N_DOM]
        assert sorted(o for o in arrived if o is not None) == wanted
        sent = sent_offsets(d)
        assert sorted(sent) == list(OFFSETS)
        row = [block_of(o) for o in sent]
        row += [sent.index(-o) for o in OFFSETS]
        row += [-1 if o is None else block_of(-o) for o in arrived]
        row += [arrived.index(o) if o in arrived else -1 for o in OFFSETS]
        rows.append(row)
    return np.array(rows, np.int32)


SENT_BLOCK, SENT_PLACE, ARRIVED_BLOCK, ARRIVED_PLACE, TABLE_WIDTH = 0, 8, 16, 28, 36


def face_nodes():
    nodes = np.zeros((6, 16), np.int32)
    for k in range(16):
        hi, lo = divmod(k, 4)
        nodes[:, k] = (4 * lo + 16 * hi, 3 + 4 * lo + 16 * hi, lo + 16 * hi, 12 + lo + 16 * hi, k, 48 + k)
    return nodes


def face_select():
    nodes = face_nodes()
    select = np.zeros((480, 320), np.float32)
    for f in range(6):
        for v in range(5):
            for k in range(16):
                select[f * 80 + v * 16 + k, v * 64 + nodes[f, k]] = 1.0
    return select


def dot(a, b):
    return lax.dot_general(a, b, (((1,), (0,)), ((), ())), preferred_element_type=F32)


def dot_t(a, b):
    return lax.dot_general(a, b, (((1,), (1,)), ((), ())), preferred_element_type=F32)


def dot_first(a, b):
    return lax.dot_general(a, b, (((0,), (0,)), ((), ())), preferred_element_type=F32)


def iota(shape, dim):
    return lax.broadcasted_iota(I32, shape, dim)


def as_one(mask):
    return jnp.where(mask, 1.0, 0.0)


def split(x):
    hi = x.astype(BF16)
    return hi, (x - hi.astype(F32)).astype(BF16)


def dom_labels(dom_send, dom_count, blocks):
    width = 32 * len(blocks)
    slots = iota((8, E), 1)
    spread = as_one(iota((8, E), 0) == slots // 32).astype(BF16)
    counts = dot(jnp.broadcast_to(dom_count.astype(F32), (8, 8)).astype(BF16), spread)
    live = as_one((slots % 32).astype(F32) < counts)
    lists = jnp.broadcast_to(dom_send, (8, E))
    row = iota((8, E), 0)
    table = jnp.where(row == 0, (lists // 256).astype(F32), jnp.where(row == 1, (lists % 256).astype(F32), 1.0))
    table = (table * live).astype(BF16)
    lanes = iota((8, width), 1)
    source = jnp.full(lanes.shape, -1, I32)
    for i, block in enumerate(blocks):
        source = jnp.where(lanes >> 5 == i, block, source)
    source = jnp.where(source >= 0, source * 32 + (lanes & 31), -1)
    pick = as_one(iota((E, width), 0) == source[0:1, :]).astype(BF16)
    found = dot(table, pick)
    label = jnp.where(found[2:3] > 0.5, found[0:1] * 256.0 + found[1:2], -1.0)
    return label.astype(I32)


def sub_labels(sub_send, sub):
    blocks = [sub_send[:, 128 * t : 128 * t + 128] for t in range(4)]
    result = []
    for k in range(4):
        block = blocks[k]
        for s in range(1, 4):
            block = jnp.where(sub == s, blocks[s ^ k], block)
        result.append(block)
    return result


def source_rows(partner, sub, places, width):
    received = partner - LOCAL
    block = received >> 5
    place = jnp.full(partner.shape, -32, I32)
    for j, group in enumerate(places):
        place = jnp.where(block == j, 32 * group, place)
    place = place + (received & 31)
    over = received - E
    over = width + (((over >> 7) ^ sub) << 7) + (over & 127)
    return jnp.where(received >= E, over, jnp.where(received >= 0, place, -1))


def low_hot(row):
    column = iota((E, 128), 0)
    parts = [as_one(column == (row[:, i : i + 128] & 255)) for i in range(0, row.shape[1], 128)]
    return jnp.concatenate(parts, axis=1).astype(BF16)


def gather(blocks, row, count):
    rows = blocks.shape[0] // count
    out = []
    for start in range(0, row.shape[1], 256):
        part = row[:, start : start + 256]
        found = dot(blocks, low_hot(part))
        taken = jnp.zeros((rows, part.shape[1]), F32)
        for b in range(count):
            taken = jnp.where(part >> 8 == b, found[rows * b : rows * b + rows], taken)
        out.append(taken)
    return out


def scatter(values, row, count):
    block = row >> 8
    spread = [values * as_one(block == b).astype(BF16) for b in range(count)]
    return dot_t(jnp.concatenate(spread, axis=0), low_hot(row))


def payload(field_b, g_hi, select_ref, partner, dom_send, dom_count, sub_send, route, sub, outs):
    traces = dot(select_ref[...], field_b).astype(BF16)
    owed = dot(select_ref[...], g_hi).astype(BF16)
    owed = jnp.concatenate([owed[80 * f : 80 * f + 80] for f in range(6)], axis=1)
    labels = dom_labels(dom_send, dom_count, route(SENT_BLOCK, 8))
    labels = jnp.concatenate([labels] + sub_labels(sub_send, sub), axis=1)
    sent = jnp.concatenate(gather(traces, labels, 6), axis=1).astype(BF16)
    places = source_rows(partner, sub, route(SENT_PLACE, 8), E)
    back = scatter(owed, places, 3).astype(BF16)
    same_ref, cross_ref, own_ref, near_ref, last_ref = outs
    for i, ref in enumerate((same_ref, cross_ref, own_ref, near_ref.at[0], near_ref.at[1], last_ref)):
        ref[0:80, :] = sent[:, 128 * i : 128 * i + 128]
        b, half = divmod(i, 2)
        ref[80:160, :] = back[80 * b : 80 * b + 80, 128 * half : 128 * half + 128]


def lifted(faces, lift_hi, lift_lo):
    hi, lo = split(faces)
    return dot(lift_hi, hi) + dot(lift_hi, lo) + dot(lift_lo, hi)


def arrived_parts(arrays, partner, dom_send, dom_count, sub_send, route, chip, sub):
    core_ref, pair_ref, even_ref, odd_ref, own_ref, near_ref, last_ref = arrays
    group = iota((160, 128), 1) // 32
    direct = jnp.where(group == 1 - chip % 2, pair_ref[0], jnp.where(group < 2, pair_ref[1], core_ref[...]))
    parts = [direct, even_ref[...], odd_ref[...], own_ref[...], near_ref[0], last_ref[1], last_ref[0]]
    traces = [jnp.concatenate([parts[2 * b][0:80], parts[min(2 * b + 1, 6)][0:80]], axis=1) for b in range(4)]
    places = source_rows(partner, sub, route(ARRIVED_PLACE, 8), 384)
    nbr = jnp.concatenate(gather(jnp.concatenate(traces, axis=0), places, 4), axis=0)
    labels = dom_labels(dom_send, dom_count, route(ARRIVED_BLOCK, 12))
    labels = jnp.concatenate([labels] + sub_labels(sub_send, sub), axis=1)
    returned = jnp.concatenate([part[80:160] for part in parts], axis=1)
    return nbr, scatter(returned, labels, 6)


def local_parts(field_b, g, select_ref, partner):
    select = select_ref[...]
    traces = dot(select, field_b)
    g_hi, g_lo = split(g)
    owed_hi, owed_lo = dot(select, g_hi), dot(select, g_lo)
    pair = jnp.concatenate(
        [jnp.concatenate([owed_hi[80 * f : 80 * f + 80], owed_lo[80 * f : 80 * f + 80]], axis=0) for f in range(6)],
        axis=1,
    ).astype(BF16)
    nbr = jnp.concatenate(gather(traces.astype(BF16), partner, 6), axis=0)
    back = scatter(pair, partner, 6)
    back = jnp.concatenate([back[160 * f : 160 * f + 80] + back[160 * f + 80 : 160 * f + 160] for f in range(6)], axis=0)
    return nbr - traces, back - (owed_hi + owed_lo)


def build_weights(in_t, mid_weight, out_weight, flux, biases, outs):
    a1, a1t, wm, wmt, a3, a3t, lift_hi, lift_lo, back_hi, back_lo, bias_ref = outs

    def mask(shape, condition, dtype=BF16):
        return as_one(condition(iota(shape, 0), iota(shape, 1))).astype(dtype)

    spread = mask((256, 64), lambda r, c: r // 4 == c)
    spread_t = mask((64, 256), lambda r, c: c // 4 == r)
    same = mask((256, 256), lambda r, c: r % 4 == c % 4, F32)
    wm[...] = (dot(dot(spread, mid_weight).astype(BF16), spread_t) * same).astype(BF16)
    wmt[...] = (dot(dot_t(spread, mid_weight).astype(BF16), spread_t) * same).astype(BF16)
    ten = mask((10, 160), lambda r, c: c // 16 == r)
    ten_t = mask((160, 10), lambda r, c: r // 16 == c)
    five = mask((5, 80), lambda r, c: c // 16 == r)
    five_t = mask((80, 5), lambda r, c: r // 16 == c)
    rows_in = dot(dot_t(spread, in_t).astype(BF16), ten)
    cols_in = dot(dot(ten_t, in_t).astype(BF16), spread_t)
    cols_out = dot(dot(five_t, out_weight).astype(BF16), spread_t)
    rows_out = dot(dot_t(spread, out_weight).astype(BF16), five)
    for s in range(4):
        a1[256 * s : 256 * s + 256, :] = (
            rows_in * mask((256, 160), lambda r, c: c % 16 == 4 * s + r % 4, F32)
        ).astype(BF16)
        a1t[:, 256 * s : 256 * s + 256] = (
            cols_in * mask((160, 256), lambda r, c: r % 16 == 4 * s + c % 4, F32)
        ).astype(BF16)
        a3[:, 256 * s : 256 * s + 256] = (
            cols_out * mask((80, 256), lambda r, c: r % 16 == 4 * s + c % 4, F32)
        ).astype(BF16)
        a3t[256 * s : 256 * s + 256, :] = (
            rows_out * mask((256, 80), lambda r, c: c % 16 == 4 * s + r % 4, F32)
        ).astype(BF16)
    ones = jnp.ones((64, 128), BF16)
    for i, bias in enumerate(biases):
        hi, rest = split(bias)
        mid, low = split(bias - hi.astype(F32))
        bias_ref[i] = dot(spread * hi, ones) + dot(spread * mid, ones) + dot(spread * low, ones)
    lane = iota((8, 480), 1)
    f, k = lane // 80, lane % 16
    hi, lo = k // 4, k % 4
    node = jnp.where(f < 2, 4 * lo + 16 * hi + 3 * f, jnp.where(f < 4, lo + 16 * hi + 12 * (f - 2), k + 48 * (f - 4)))
    meets = as_one(iota((320, 480), 0) % 64 == node[0:1])
    var = mask((320, 5), lambda r, c: r // 64 == c)
    var_t = mask((5, 480), lambda r, c: (c % 80) // 16 == r)
    for part, forward, backward in zip(split(GAIN * flux), (lift_hi, lift_lo), (back_hi, back_lo)):
        forward[...] = (dot(dot(var, part).astype(BF16), var_t) * meets).astype(BF16)
        backward[...] = (dot(dot_t(var, part).astype(BF16), var_t) * meets).astype(BF16)


def wide(bias):
    return jnp.concatenate([bias, bias], axis=1)


def quarter(s):
    return slice(256 * s, 256 * s + 256)


def group_rows(ref, start):
    return jnp.concatenate([ref[pl.ds(64 * v + start, 16), :] for v in range(5)], axis=0)


def group_inputs(field_ref, volume_ref, start):
    return jnp.concatenate([group_rows(field_ref, start), group_rows(volume_ref, start)], axis=0)


def route_of(place_ref, table_ref):
    row = place_ref[0] * TABLE_WIDTH

    def route(start, count):
        return [table_ref[row + start + i] for i in range(count)]

    return route


def first_kernel(place_ref, table_ref, *refs):
    count = (len(refs) - 6) // 2
    sources, copies, sems = refs[:count], refs[count : 2 * count], refs[-1]
    outs = refs[2 * count : -1]
    moves = [pltpu.make_async_copy(a, b, sems.at[i]) for i, (a, b) in enumerate(zip(sources, copies))]
    for move in moves:
        move.start()
    for move in moves[:7]:
        move.wait()
    init_ref, cot_ref, select_ref, partner_ref, dom_send_ref, dom_count_ref, sub_send_ref = copies[:7]
    payload(
        init_ref[...].astype(BF16), cot_ref[...].astype(BF16), select_ref, partner_ref[...],
        dom_send_ref[...], dom_count_ref[...], sub_send_ref[...], route_of(place_ref, table_ref), place_ref[1], outs,
    )
    for move in moves[7:]:
        move.wait()


def second_kernel(
    init_ref, cot_ref, select_ref, partner_ref, volume_op_ref, in_ref, mid_ref, out_ref, flux_ref,
    in_bias_ref, mid_bias_ref,
    part_ref, adj_ref, slope1_ref, slope2_ref, a1, a1t, wm, wmt, a3, a3t, lift_hi, lift_lo, back_hi, back_lo, bias_ref,
    field_s, volume_s, h_s,
):
    build_weights(
        in_ref[...], mid_ref[...], out_ref[...], flux_ref[...], (in_bias_ref[...], mid_bias_ref[...]),
        (a1, a1t, wm, wmt, a3, a3t, lift_hi, lift_lo, back_hi, back_lo, bias_ref),
    )
    field_b = init_ref[...].astype(BF16)
    jump, trace_grad = local_parts(field_b, cot_ref[...], select_ref, partner_ref[...])
    adj_ref[...] = 0.5 * cot_ref[...] + (0.5 * STEP) * lifted(trace_grad, back_hi[...], back_lo[...])
    volume = dot(volume_op_ref[...], field_b)
    part_ref[...] = init_ref[...] + STEP * (volume + lifted(jump, lift_hi[...], lift_lo[...]))
    field_s[...] = field_b
    volume_s[...] = volume.astype(BF16)

    def group(i, carry):
        start = pl.multiple_of(16 * i, 16)
        inputs = group_inputs(field_s, volume_s, start)
        for s in range(4):
            h1 = jnp.tanh(dot(a1[quarter(s), :], inputs) + wide(bias_ref[0]))
            h_s[0, quarter(s), :] = h1.astype(BF16)
            slope1_ref[i, quarter(s), :] = (1.0 - h1 * h1).astype(BF16)
        for s in range(4):
            h2 = jnp.tanh(dot(wm[...], h_s[0, quarter(s), :]) + wide(bias_ref[1]))
            h_s[1, quarter(s), :] = h2.astype(BF16)
            slope2_ref[i, quarter(s), :] = (1.0 - h2 * h2).astype(BF16)
        out = dot(a3[...], h_s[1])
        for v in range(5):
            rows = pl.ds(64 * v + start, 16)
            part_ref[rows, :] = part_ref[rows, :] + STEP * out[16 * v : 16 * v + 16]
        return carry

    lax.fori_loop(0, 4, group, 0)


def third_kernel(place_ref, table_ref, *refs):
    arrays, refs = refs[:7], refs[7:]
    (
        part_ref, adj_part_ref, cot_ref, select_ref, partner_ref,
        dom_send_ref, dom_count_ref, sub_send_ref, volume_op_ref,
        a1, a1t, wm, wmt, a3, a3t, lift_hi, lift_lo, back_hi, back_lo, bias_ref,
        middle_ref, base_ref, adj_ref, *sent_refs,
    ) = refs[:28]
    field_s, volume_s, cot_s, fgrad_s, vgrad_s, h_s, slope_s, delta_s = refs[28:]
    route, sub = route_of(place_ref, table_ref), place_ref[1]
    partner, dom_send, dom_count, sub_send = partner_ref[...], dom_send_ref[...], dom_count_ref[...], sub_send_ref[...]
    nbr, back = arrived_parts(arrays, partner, dom_send, dom_count, sub_send, route, place_ref[0] >> 1, sub)
    nbr_b = nbr.astype(BF16)
    middle = part_ref[...] + STEP * (dot(lift_hi[...], nbr_b) + dot(lift_lo[...], nbr_b))
    middle_ref[...] = middle
    adj_ref[...] = adj_part_ref[...] + (0.5 * STEP) * lifted(back, back_hi[...], back_lo[...])
    field_b = middle.astype(BF16)
    volume = dot(volume_op_ref[...], field_b)
    base_ref[...] = volume
    field_s[...] = field_b
    volume_s[...] = volume.astype(BF16)
    cot_s[...] = cot_ref[...].astype(BF16)

    def group(i, carry):
        start = pl.multiple_of(16 * i, 16)
        inputs = group_inputs(field_s, volume_s, start)
        upstream = group_rows(cot_s, start)
        for s in range(4):
            h1 = jnp.tanh(dot(a1[quarter(s), :], inputs) + wide(bias_ref[0]))
            h_s[0, quarter(s), :] = h1.astype(BF16)
            slope_s[quarter(s), :] = 1.0 - h1 * h1
        for s in range(4):
            h2 = jnp.tanh(dot(wm[...], h_s[0, quarter(s), :]) + wide(bias_ref[1]))
            h_s[1, quarter(s), :] = h2.astype(BF16)
            delta_s[0, quarter(s), :] = (dot(a3t[quarter(s), :], upstream) * (1.0 - h2 * h2)).astype(BF16)
        out = dot(a3[...], h_s[1])
        for s in range(4):
            delta_s[1, quarter(s), :] = (dot(wmt[...], delta_s[0, quarter(s), :]) * slope_s[quarter(s), :]).astype(BF16)
        grad = dot(a1t[...], delta_s[1])
        for v in range(5):
            rows = pl.ds(64 * v + start, 16)
            base_ref[rows, :] = base_ref[rows, :] + out[16 * v : 16 * v + 16]
            fgrad_s[rows, :] = grad[16 * v : 16 * v + 16]
            vgrad_s[rows, :] = grad[80 + 16 * v : 96 + 16 * v]
        return carry

    lax.fori_loop(0, 4, group, 0)
    total = (cot_ref[...] + vgrad_s[...]).astype(BF16)
    adj = adj_ref[...] + (0.5 * STEP) * (dot_first(volume_op_ref[...], total) + fgrad_s[...])
    adj_ref[...] = adj
    payload(field_b, adj.astype(BF16), select_ref, partner, dom_send, dom_count, sub_send, route, sub, sent_refs)


def fourth_kernel(
    init_ref, cot_ref, middle_ref, base_ref, adj_ref, select_ref, partner_ref, volume_op_ref,
    slope1_ref, slope2_ref, a1t, wmt, a3t, lift_hi, lift_lo, back_hi, back_lo,
    fin_ref, out_ref, adj_s, fgrad_s, vgrad_s, delta_s,
):
    middle, adj = middle_ref[...], adj_ref[...]
    jump, trace_grad = local_parts(middle.astype(BF16), adj, select_ref, partner_ref[...])
    residual = base_ref[...] + lifted(jump, lift_hi[...], lift_lo[...])
    fin_ref[...] = 0.5 * init_ref[...] + 0.5 * (middle + STEP * residual)
    out_ref[...] = lifted(trace_grad, back_hi[...], back_lo[...])
    adj_s[...] = adj.astype(BF16)

    def group(i, carry):
        start = pl.multiple_of(16 * i, 16)
        upstream = group_rows(adj_s, start)
        for s in range(4):
            delta = dot(a3t[quarter(s), :], upstream) * slope2_ref[i, quarter(s), :].astype(F32)
            delta_s[0, quarter(s), :] = delta.astype(BF16)
        for s in range(4):
            delta = dot(wmt[...], delta_s[0, quarter(s), :]) * slope1_ref[i, quarter(s), :].astype(F32)
            delta_s[1, quarter(s), :] = delta.astype(BF16)
        grad = dot(a1t[...], delta_s[1])
        for v in range(5):
            rows = pl.ds(64 * v + start, 16)
            fgrad_s[rows, :] = grad[16 * v : 16 * v + 16]
            vgrad_s[rows, :] = grad[80 + 16 * v : 96 + 16 * v]
        return carry

    lax.fori_loop(0, 4, group, 0)
    adj = adj_ref[...]
    total = (adj + vgrad_s[...]).astype(BF16)
    local = dot_first(volume_op_ref[...], total) + fgrad_s[...] + out_ref[...]
    out_ref[...] = 0.5 * cot_ref[...] + adj + STEP * local


def fifth_kernel(place_ref, table_ref, *refs):
    arrays, refs = refs[:7], refs[7:]
    (
        fin_part_ref, out_part_ref, partner_ref, dom_send_ref, dom_count_ref, sub_send_ref,
        lift_hi, lift_lo, back_hi, back_lo, fin_ref, out_ref,
    ) = refs
    nbr, back = arrived_parts(
        arrays, partner_ref[...], dom_send_ref[...], dom_count_ref[...], sub_send_ref[...],
        route_of(place_ref, table_ref), place_ref[0] >> 1, place_ref[1],
    )
    nbr_b = nbr.astype(BF16)
    fin_ref[...] = fin_part_ref[...] + (0.5 * STEP) * (dot(lift_hi[...], nbr_b) + dot(lift_lo[...], nbr_b))
    out_ref[...] = out_part_ref[...] + STEP * lifted(back, back_hi[...], back_lo[...])


def call(kernel, name, outs, inputs, scratch=(), scalars=0, cost=None, final=False, raw=False):
    specs = [pl.BlockSpec(memory_space=pltpu.SMEM)] * scalars
    specs += [pl.BlockSpec(memory_space=pltpu.HBM if raw else pltpu.VMEM)] * (len(inputs) - scalars)
    kind = jax.ShapeDtypeStruct if final else pltpu.VMEM
    if scalars:
        inputs = (inputs[0], pltpu.with_memory_space_constraint(inputs[1], pltpu.HBM)) + tuple(inputs[2:])
    if raw:
        inputs = inputs[:scalars] + tuple(pltpu.with_memory_space_constraint(x, pltpu.HBM) for x in inputs[scalars:])
        scratch = [pltpu.SemaphoreType.DMA((len(inputs) - scalars,))]
    else:
        scratch = [pltpu.VMEM(shape, dtype) for shape, dtype in scratch]
    return pl.pallas_call(
        kernel,
        name=name,
        out_shape=[kind(shape, dtype) for shape, dtype in outs],
        in_specs=specs,
        out_specs=[pl.BlockSpec(memory_space=pltpu.VMEM)] * len(outs),
        scratch_shapes=scratch,
        cost_estimate=cost,
        compiler_params=pltpu.CompilerParams(vmem_limit_bytes=30 * 1024 * 1024),
    )(*inputs)


PAYLOAD = [((160, 128), BF16)] * 3 + [((2, 160, 128), BF16), ((160, 128), BF16)]
STATE = ((320, E), F32)
STATE_B = ((320, E), BF16)
MATRICES = [
    ((1024, 160), BF16), ((160, 1024), BF16), ((256, 256), BF16), ((256, 256), BF16),
    ((80, 1024), BF16), ((1024, 80), BF16),
    ((320, 480), BF16), ((320, 480), BF16), ((320, 480), BF16), ((320, 480), BF16), ((2, 256, 128), F32),
]
PAIR = ((2, 1024, E), BF16)
COST = pl.CostEstimate(flops=10_000_000_000, transcendentals=0, bytes_accessed=8_000_000)


def exchange(place, same, cross, own, near, last):
    def hop(x, target):
        return lax.ppermute(x, "dom", [(d, target(d)) for d in range(N_DOM)])

    def swap(x, k):
        return lax.ppermute(x, "sub", [(i, i ^ k) for i in range(4)])

    core = hop(cross, to_core)
    near = swap(near, 1)
    pair = hop(jnp.stack([same, core]), to_pair)
    last = swap(jnp.stack([last, near[1]]), 3)
    group = iota((160, 128), 1) // 32
    up = jnp.where(group == 0, same, jnp.where(group == 1, core, jnp.where(group == 2, pair[0], pair[1])))
    down = jnp.where(group == 0, core, jnp.where(group == 1, same, jnp.where(group == 2, pair[1], pair[0])))
    first = ((place[0] >> 2) & 1) == 0
    even = hop(jnp.where(first, up, down), reversed_even)
    odd = hop(jnp.where(first, down, up), reversed_odd)
    return core, pair, even, odd, own, near, last


def body(
    initial_state, cotangent, volume_operator, in_weight, in_bias, mid_weight, mid_bias, out_weight, flux_matrix,
    dom_send, dom_count, sub_send, partner,
):
    select = jnp.asarray(face_select(), BF16)
    table = jnp.asarray(routing_tables().reshape(-1))
    place = jnp.stack([lax.axis_index("dom"), lax.axis_index("sub")]).astype(I32)
    raw = (
        initial_state, cotangent, select, partner, dom_send, dom_count, sub_send,
        volume_operator, in_weight.T, mid_weight, out_weight, flux_matrix, in_bias.reshape(1, 64), mid_bias.reshape(1, 64),
    )
    copies = [(x.shape, x.dtype) for x in raw]
    done = call(first_kernel, "first", copies + PAYLOAD, (place, table) + raw, scalars=2, raw=True)
    initial_state, cotangent, select, partner, dom_send, dom_count, sub_send, volume_operator = done[:8]
    lists = (partner, dom_send, dom_count, sub_send)
    arrived = exchange(place, *done[len(raw):])
    part, adj_part, slope1, slope2, *mats = call(
        second_kernel, "second",
        [STATE, STATE, ((4, 1024, E), BF16), ((4, 1024, E), BF16)] + MATRICES,
        (initial_state, cotangent, select, partner, *done[7 : len(raw)]),
        [STATE_B, STATE_B, PAIR], cost=COST,
    )
    a1, a1t, wm, wmt, a3, a3t, *lifts, bias = mats
    middle, base, adj, *sent = call(
        third_kernel, "third", [STATE, STATE, STATE] + PAYLOAD,
        (place, table, *arrived, part, adj_part, cotangent, select, *lists, volume_operator, *mats),
        [STATE_B, STATE_B, STATE_B, STATE, STATE, PAIR, ((1024, E), F32), PAIR], scalars=2,
    )
    arrived = exchange(place, *sent)
    fin_part, out_part = call(
        fourth_kernel, "fourth", [STATE, STATE],
        (
            initial_state, cotangent, middle, base, adj, select, partner, volume_operator, slope1, slope2,
            a1t, wmt, a3t, *lifts,
        ),
        [STATE_B, STATE, STATE, PAIR], cost=COST,
    )
    final_state, adjoint_state = call(
        fifth_kernel, "fifth", [STATE, STATE],
        (place, table, *arrived, fin_part, out_part, *lists, *lifts), scalars=2, final=True,
    )
    return final_state, adjoint_state


def solution(mesh):
    columns = P(None, ("dom", "sub"))
    pairs = P("dom", "sub")
    return jax.shard_map(
        body,
        mesh=mesh,
        in_specs=(columns, columns, P(), P(), P(), P(), P(), P(), P(), pairs, pairs, pairs, pairs),
        out_specs=(columns, columns),
        check_vma=False,
    )
```

```python
import jax
import jax.numpy as jnp
import numpy as np
from jax import lax
from jax.experimental import pallas as pl
from jax.experimental.pallas import tpu as pltpu
from jax.sharding import PartitionSpec as P

E = 256
LOCAL = 6 * E
OFFSETS = (-4, -3, -2, -1, 1, 2, 3, 4)
N_DOM = 64
STEP = 0.4
GAIN = 1.5
F32, BF16, I32 = jnp.float32, jnp.bfloat16, jnp.int32


def block_of(offset):
    return OFFSETS.index(offset)


def to_core(d):
    return d ^ 1


def to_pair(d):
    return d ^ 2


def reversed_even(d):
    return d ^ 6


def reversed_odd(d):
    chip, core = divmod(d, 2)
    other = ((chip + 2) ^ 3) - 2
    return 2 * other + core if 0 <= other < N_DOM // 2 else d


def sent_offsets(d):
    return (2, -2, 4, -4) + ((-3, 1, -1, 3) if d % 2 else (-1, 3, -3, 1))


def routing_tables():
    hold = {d: [(d, o) for o in sent_offsets(d)] for d in range(N_DOM)}
    core = {d: hold[to_core(d)][4:] for d in range(N_DOM)}
    even, odd, direct = {}, {}, {}
    for d in range(N_DOM):
        same, other = hold[to_pair(d)][:4], core[to_pair(d)]
        up = [hold[d][0], core[d][1], same[2], other[3]]
        down = [core[d][0], hold[d][1], other[2], same[3]]
        even[d], odd[d] = (down, up) if d // 4 % 2 else (up, down)
        direct[d] = ([same[0], other[1]] if d // 2 % 2 else [other[0], same[1]]) + core[d][2:]
    rows = []
    for d in range(N_DOM):
        found = direct[d] + even[reversed_even(d)] + odd[reversed_odd(d)]
        arrived = [None] * 12
        for i, item in enumerate(found):
            if item[0] != d and sum(item) == d and item[1] not in arrived:
                arrived[i] = item[1]
        wanted = [o for o in OFFSETS if 0 <= d - o < N_DOM]
        assert sorted(o for o in arrived if o is not None) == wanted
        sent = sent_offsets(d)
        assert sorted(sent) == list(OFFSETS)
        row = [block_of(o) for o in sent]
        row += [sent.index(-o) for o in OFFSETS]
        row += [-1 if o is None else block_of(-o) for o in arrived]
        row += [arrived.index(o) if o in arrived else -1 for o in OFFSETS]
        rows.append(row)
    return np.array(rows, np.int32)


SENT_BLOCK, SENT_PLACE, ARRIVED_BLOCK, ARRIVED_PLACE, TABLE_WIDTH = 0, 8, 16, 28, 36


def face_nodes():
    nodes = np.zeros((6, 16), np.int32)
    for k in range(16):
        hi, lo = divmod(k, 4)
        nodes[:, k] = (4 * lo + 16 * hi, 3 + 4 * lo + 16 * hi, lo + 16 * hi, 12 + lo + 16 * hi, k, 48 + k)
    return nodes


def face_select():
    nodes = face_nodes()
    select = np.zeros((480, 320), np.float32)
    for f in range(6):
        for v in range(5):
            for k in range(16):
                select[f * 80 + v * 16 + k, v * 64 + nodes[f, k]] = 1.0
    return select


def dot(a, b):
    return lax.dot_general(a, b, (((1,), (0,)), ((), ())), preferred_element_type=F32)


def dot_t(a, b):
    return lax.dot_general(a, b, (((1,), (1,)), ((), ())), preferred_element_type=F32)


def dot_first(a, b):
    return lax.dot_general(a, b, (((0,), (0,)), ((), ())), preferred_element_type=F32)


def iota(shape, dim):
    return lax.broadcasted_iota(I32, shape, dim)


def as_one(mask):
    return jnp.where(mask, 1.0, 0.0)


def split(x):
    hi = x.astype(BF16)
    return hi, (x - hi.astype(F32)).astype(BF16)


def dom_labels(dom_send, dom_count, blocks):
    width = 32 * len(blocks)
    slots = iota((8, E), 1)
    spread = as_one(iota((8, E), 0) == slots // 32).astype(BF16)
    counts = dot(jnp.broadcast_to(dom_count.astype(F32), (8, 8)).astype(BF16), spread)
    live = as_one((slots % 32).astype(F32) < counts)
    lists = jnp.broadcast_to(dom_send, (8, E))
    row = iota((8, E), 0)
    table = jnp.where(row == 0, (lists // 256).astype(F32), jnp.where(row == 1, (lists % 256).astype(F32), 1.0))
    table = (table * live).astype(BF16)
    lanes = iota((8, width), 1)
    source = jnp.full(lanes.shape, -1, I32)
    for i, block in enumerate(blocks):
        source = jnp.where(lanes >> 5 == i, block, source)
    source = jnp.where(source >= 0, source * 32 + (lanes & 31), -1)
    pick = as_one(iota((E, width), 0) == source[0:1, :]).astype(BF16)
    found = dot(table, pick)
    label = jnp.where(found[2:3] > 0.5, found[0:1] * 256.0 + found[1:2], -1.0)
    return label.astype(I32)


def sub_labels(sub_send, sub):
    blocks = [sub_send[:, 128 * t : 128 * t + 128] for t in range(4)]
    result = []
    for k in range(4):
        block = blocks[k]
        for s in range(1, 4):
            block = jnp.where(sub == s, blocks[s ^ k], block)
        result.append(block)
    return result


def source_rows(partner, sub, places, width):
    received = partner - LOCAL
    block = received >> 5
    place = jnp.full(partner.shape, -32, I32)
    for j, group in enumerate(places):
        place = jnp.where(block == j, 32 * group, place)
    place = place + (received & 31)
    over = received - E
    over = width + (((over >> 7) ^ sub) << 7) + (over & 127)
    return jnp.where(received >= E, over, jnp.where(received >= 0, place, -1))


def low_hot(row):
    column = iota((E, 128), 0)
    parts = [as_one(column == (row[:, i : i + 128] & 255)) for i in range(0, row.shape[1], 128)]
    return jnp.concatenate(parts, axis=1).astype(BF16)


def gather(blocks, row, count):
    rows = blocks.shape[0] // count
    out = []
    for start in range(0, row.shape[1], 256):
        part = row[:, start : start + 256]
        found = dot(blocks, low_hot(part))
        taken = jnp.zeros((rows, part.shape[1]), F32)
        for b in range(count):
            taken = jnp.where(part >> 8 == b, found[rows * b : rows * b + rows], taken)
        out.append(taken)
    return out


def scatter(values, row, count):
    block = row >> 8
    spread = [values * as_one(block == b).astype(BF16) for b in range(count)]
    return dot_t(jnp.concatenate(spread, axis=0), low_hot(row))


def payload_plan(partner, dom_send, dom_count, sub_send, route, sub):
    labels = dom_labels(dom_send, dom_count, route(SENT_BLOCK, 8))
    labels = jnp.concatenate([labels] + sub_labels(sub_send, sub), axis=1)
    return labels, source_rows(partner, sub, route(SENT_PLACE, 8), E)


def payload(field_b, g_hi, select_ref, plan, outs):
    labels, places = plan
    traces = dot(select_ref[...], field_b).astype(BF16)
    owed = dot(select_ref[...], g_hi).astype(BF16)
    owed = jnp.concatenate([owed[80 * f : 80 * f + 80] for f in range(6)], axis=1)
    sent = jnp.concatenate(gather(traces, labels, 6), axis=1).astype(BF16)
    back = scatter(owed, places, 3).astype(BF16)
    same_ref, cross_ref, own_ref, near_ref, last_ref = outs
    for i, ref in enumerate((same_ref, cross_ref, own_ref, near_ref.at[0], near_ref.at[1], last_ref)):
        ref[0:80, :] = sent[:, 128 * i : 128 * i + 128]
        b, half = divmod(i, 2)
        ref[80:160, :] = back[80 * b : 80 * b + 80, 128 * half : 128 * half + 128]


def lifted(faces, lift_hi, lift_lo):
    hi, lo = split(faces)
    return dot(lift_hi, hi) + dot(lift_hi, lo) + dot(lift_lo, hi)


def arrived_parts(arrays, partner, dom_send, dom_count, sub_send, route, chip, sub):
    core_ref, pair_ref, even_ref, odd_ref, own_ref, near_ref, last_ref = arrays
    group = iota((160, 128), 1) // 32
    direct = jnp.where(group == 1 - chip % 2, pair_ref[0], jnp.where(group < 2, pair_ref[1], core_ref[...]))
    parts = [direct, even_ref[...], odd_ref[...], own_ref[...], near_ref[0], last_ref[1], last_ref[0]]
    traces = [jnp.concatenate([parts[2 * b][0:80], parts[min(2 * b + 1, 6)][0:80]], axis=1) for b in range(4)]
    places = source_rows(partner, sub, route(ARRIVED_PLACE, 8), 384)
    nbr = jnp.concatenate(gather(jnp.concatenate(traces, axis=0), places, 4), axis=0)
    labels = dom_labels(dom_send, dom_count, route(ARRIVED_BLOCK, 12))
    labels = jnp.concatenate([labels] + sub_labels(sub_send, sub), axis=1)
    returned = jnp.concatenate([part[80:160] for part in parts], axis=1)
    return nbr, scatter(returned, labels, 6)


def local_jump(field_b, select_ref, partner):
    traces = dot(select_ref[...], field_b)
    return jnp.concatenate(gather(traces.astype(BF16), partner, 6), axis=0) - traces


def local_trace(g, select_ref, partner):
    select = select_ref[...]
    g_hi, g_lo = split(g)
    owed_hi, owed_lo = dot(select, g_hi), dot(select, g_lo)
    pair = jnp.concatenate(
        [jnp.concatenate([owed_hi[80 * f : 80 * f + 80], owed_lo[80 * f : 80 * f + 80]], axis=0) for f in range(6)],
        axis=1,
    ).astype(BF16)
    back = scatter(pair, partner, 6)
    back = jnp.concatenate([back[160 * f : 160 * f + 80] + back[160 * f + 80 : 160 * f + 160] for f in range(6)], axis=0)
    return back - (owed_hi + owed_lo)


def build_weights(in_t, mid_weight, out_weight, flux, biases, outs):
    a1, a1t, wm, wmt, a3, a3t, lift_hi, lift_lo, back_hi, back_lo, bias_ref = outs

    def mask(shape, condition, dtype=BF16):
        return as_one(condition(iota(shape, 0), iota(shape, 1))).astype(dtype)

    spread = mask((256, 64), lambda r, c: r // 4 == c)
    spread_t = mask((64, 256), lambda r, c: c // 4 == r)
    same = mask((256, 256), lambda r, c: r % 4 == c % 4, F32)
    wm[...] = (dot(dot(spread, mid_weight).astype(BF16), spread_t) * same).astype(BF16)
    wmt[...] = (dot(dot_t(spread, mid_weight).astype(BF16), spread_t) * same).astype(BF16)
    ten = mask((10, 160), lambda r, c: c // 16 == r)
    ten_t = mask((160, 10), lambda r, c: r // 16 == c)
    five = mask((5, 80), lambda r, c: c // 16 == r)
    five_t = mask((80, 5), lambda r, c: r // 16 == c)
    rows_in = dot(dot_t(spread, in_t).astype(BF16), ten)
    cols_in = dot(dot(ten_t, in_t).astype(BF16), spread_t)
    cols_out = dot(dot(five_t, out_weight).astype(BF16), spread_t)
    rows_out = dot(dot_t(spread, out_weight).astype(BF16), five)
    for s in range(4):
        a1[256 * s : 256 * s + 256, :] = (
            rows_in * mask((256, 160), lambda r, c: c % 16 == 4 * s + r % 4, F32)
        ).astype(BF16)
        a1t[:, 256 * s : 256 * s + 256] = (
            cols_in * mask((160, 256), lambda r, c: r % 16 == 4 * s + c % 4, F32)
        ).astype(BF16)
        a3[:, 256 * s : 256 * s + 256] = (
            cols_out * mask((80, 256), lambda r, c: r % 16 == 4 * s + c % 4, F32)
        ).astype(BF16)
        a3t[256 * s : 256 * s + 256, :] = (
            rows_out * mask((256, 80), lambda r, c: c % 16 == 4 * s + r % 4, F32)
        ).astype(BF16)
    ones = jnp.ones((64, 128), BF16)
    for i, bias in enumerate(biases):
        hi, rest = split(bias)
        mid, low = split(bias - hi.astype(F32))
        bias_ref[i] = dot(spread * hi, ones) + dot(spread * mid, ones) + dot(spread * low, ones)
    lane = iota((8, 480), 1)
    f, k = lane // 80, lane % 16
    hi, lo = k // 4, k % 4
    node = jnp.where(f < 2, 4 * lo + 16 * hi + 3 * f, jnp.where(f < 4, lo + 16 * hi + 12 * (f - 2), k + 48 * (f - 4)))
    meets = as_one(iota((320, 480), 0) % 64 == node[0:1])
    var = mask((320, 5), lambda r, c: r // 64 == c)
    var_t = mask((5, 480), lambda r, c: (c % 80) // 16 == r)
    for part, forward, backward in zip(split(GAIN * flux), (lift_hi, lift_lo), (back_hi, back_lo)):
        forward[...] = (dot(dot(var, part).astype(BF16), var_t) * meets).astype(BF16)
        backward[...] = (dot(dot_t(var, part).astype(BF16), var_t) * meets).astype(BF16)


def wide(bias):
    return jnp.concatenate([bias, bias], axis=1)


def quarter(s):
    return slice(256 * s, 256 * s + 256)


def group_rows(ref, start):
    return jnp.concatenate([ref[pl.ds(64 * v + start, 16), :] for v in range(5)], axis=0)


def group_inputs(field_ref, volume_ref, start):
    return jnp.concatenate([group_rows(field_ref, start), group_rows(volume_ref, start)], axis=0)


def route_of(place_ref, table_ref):
    row = place_ref[0] * TABLE_WIDTH

    def route(start, count):
        return [table_ref[row + start + i] for i in range(count)]

    return route


def first_kernel(place_ref, table_ref, *refs):
    count = (len(refs) - 6) // 2
    sources, copies, sems = refs[:count], refs[count : 2 * count], refs[-1]
    outs = refs[2 * count : -1]
    moves = [pltpu.make_async_copy(a, b, sems.at[i]) for i, (a, b) in enumerate(zip(sources, copies))]
    for move in moves:
        move.start()
    init_ref, cot_ref, select_ref, partner_ref, dom_send_ref, dom_count_ref, sub_send_ref = copies[:7]
    for move in moves[3:7]:
        move.wait()
    route, sub = route_of(place_ref, table_ref), place_ref[1]
    plan = payload_plan(partner_ref[...], dom_send_ref[...], dom_count_ref[...], sub_send_ref[...], route, sub)
    for move in moves[:3]:
        move.wait()
    payload(init_ref[...].astype(BF16), cot_ref[...].astype(BF16), select_ref, plan, outs)
    for move in moves[7:]:
        move.wait()


def weights_kernel(in_ref, mid_ref, out_ref, flux_ref, in_bias_ref, mid_bias_ref, *outs):
    build_weights(in_ref[...], mid_ref[...], out_ref[...], flux_ref[...], (in_bias_ref[...], mid_bias_ref[...]), outs)


def second_kernel(
    init_ref, cot_ref, select_ref, partner_ref, volume_op_ref, a1, wm, a3, lift_hi, lift_lo, back_hi, back_lo, bias_ref,
    part_ref, adj_ref, slope1_ref, slope2_ref, field_s, volume_s, h_s,
):
    field_b = init_ref[...].astype(BF16)
    trace_grad = local_trace(cot_ref[...], select_ref, partner_ref[...])
    adj_ref[...] = 0.5 * cot_ref[...] + (0.5 * STEP) * lifted(trace_grad, back_hi[...], back_lo[...])
    jump = local_jump(field_b, select_ref, partner_ref[...])
    volume = dot(volume_op_ref[...], field_b)
    part_ref[...] = init_ref[...] + STEP * (volume + lifted(jump, lift_hi[...], lift_lo[...]))
    field_s[...] = field_b
    volume_s[...] = volume.astype(BF16)

    def group(i, carry):
        start = pl.multiple_of(16 * i, 16)
        inputs = group_inputs(field_s, volume_s, start)
        for s in range(4):
            h1 = jnp.tanh(dot(a1[quarter(s), :], inputs) + wide(bias_ref[0]))
            h_s[0, quarter(s), :] = h1.astype(BF16)
            slope1_ref[i, quarter(s), :] = (1.0 - h1 * h1).astype(BF16)
        for s in range(4):
            h2 = jnp.tanh(dot(wm[...], h_s[0, quarter(s), :]) + wide(bias_ref[1]))
            h_s[1, quarter(s), :] = h2.astype(BF16)
            slope2_ref[i, quarter(s), :] = (1.0 - h2 * h2).astype(BF16)
        out = dot(a3[...], h_s[1])
        for v in range(5):
            rows = pl.ds(64 * v + start, 16)
            part_ref[rows, :] = part_ref[rows, :] + STEP * out[16 * v : 16 * v + 16]
        return carry

    lax.fori_loop(0, 4, group, 0)


def third_kernel(place_ref, table_ref, *refs):
    arrays, refs = refs[:7], refs[7:]
    (
        part_ref, adj_part_ref, cot_ref, select_ref, partner_ref,
        dom_send_ref, dom_count_ref, sub_send_ref, volume_op_ref,
        a1, a1t, wm, wmt, a3, a3t, lift_hi, lift_lo, back_hi, back_lo, bias_ref,
        middle_ref, base_ref, adj_ref, *sent_refs,
    ) = refs[:28]
    field_s, volume_s, cot_s, fgrad_s, vgrad_s, h_s, slope_s, delta_s = refs[28:]
    route, sub = route_of(place_ref, table_ref), place_ref[1]
    partner, dom_send, dom_count, sub_send = partner_ref[...], dom_send_ref[...], dom_count_ref[...], sub_send_ref[...]
    nbr, back = arrived_parts(arrays, partner, dom_send, dom_count, sub_send, route, place_ref[0] >> 1, sub)
    nbr_b = nbr.astype(BF16)
    middle = part_ref[...] + STEP * (dot(lift_hi[...], nbr_b) + dot(lift_lo[...], nbr_b))
    middle_ref[...] = middle
    adj_ref[...] = adj_part_ref[...] + (0.5 * STEP) * lifted(back, back_hi[...], back_lo[...])
    field_b = middle.astype(BF16)
    volume = dot(volume_op_ref[...], field_b)
    base_ref[...] = volume
    field_s[...] = field_b
    volume_s[...] = volume.astype(BF16)
    cot_s[...] = cot_ref[...].astype(BF16)

    def group(i, carry):
        start = pl.multiple_of(16 * i, 16)
        inputs = group_inputs(field_s, volume_s, start)
        upstream = group_rows(cot_s, start)
        for s in range(4):
            h1 = jnp.tanh(dot(a1[quarter(s), :], inputs) + wide(bias_ref[0]))
            h_s[0, quarter(s), :] = h1.astype(BF16)
            slope_s[quarter(s), :] = 1.0 - h1 * h1
        for s in range(4):
            h2 = jnp.tanh(dot(wm[...], h_s[0, quarter(s), :]) + wide(bias_ref[1]))
            h_s[1, quarter(s), :] = h2.astype(BF16)
            delta_s[0, quarter(s), :] = (dot(a3t[quarter(s), :], upstream) * (1.0 - h2 * h2)).astype(BF16)
        out = dot(a3[...], h_s[1])
        for s in range(4):
            delta_s[1, quarter(s), :] = (dot(wmt[...], delta_s[0, quarter(s), :]) * slope_s[quarter(s), :]).astype(BF16)
        grad = dot(a1t[...], delta_s[1])
        for v in range(5):
            rows = pl.ds(64 * v + start, 16)
            base_ref[rows, :] = base_ref[rows, :] + out[16 * v : 16 * v + 16]
            fgrad_s[rows, :] = grad[16 * v : 16 * v + 16]
            vgrad_s[rows, :] = grad[80 + 16 * v : 96 + 16 * v]
        return carry

    lax.fori_loop(0, 4, group, 0, unroll=True)
    total = (cot_ref[...] + vgrad_s[...]).astype(BF16)
    adj = adj_ref[...] + (0.5 * STEP) * (dot_first(volume_op_ref[...], total) + fgrad_s[...])
    adj_ref[...] = adj
    plan = payload_plan(partner, dom_send, dom_count, sub_send, route, sub)
    payload(field_b, adj.astype(BF16), select_ref, plan, sent_refs)


def jump_kernel(init_ref, middle_ref, base_ref, select_ref, partner_ref, lift_hi, lift_lo, fin_ref):
    middle = middle_ref[...]
    jump = local_jump(middle.astype(BF16), select_ref, partner_ref[...])
    residual = base_ref[...] + lifted(jump, lift_hi[...], lift_lo[...])
    fin_ref[...] = 0.5 * init_ref[...] + 0.5 * (middle + STEP * residual)


def fourth_kernel(
    cot_ref, adj_ref, select_ref, partner_ref, volume_op_ref, slope1_ref, slope2_ref, a1t, wmt, a3t, back_hi, back_lo,
    out_ref, adj_s, fgrad_s, vgrad_s, delta_s,
):
    adj = adj_ref[...]
    trace_grad = local_trace(adj, select_ref, partner_ref[...])
    out_ref[...] = lifted(trace_grad, back_hi[...], back_lo[...])
    adj_s[...] = adj.astype(BF16)

    def group(i, carry):
        start = pl.multiple_of(16 * i, 16)
        upstream = group_rows(adj_s, start)
        for s in range(4):
            delta = dot(a3t[quarter(s), :], upstream) * slope2_ref[i, quarter(s), :].astype(F32)
            delta_s[0, quarter(s), :] = delta.astype(BF16)
        for s in range(4):
            delta = dot(wmt[...], delta_s[0, quarter(s), :]) * slope1_ref[i, quarter(s), :].astype(F32)
            delta_s[1, quarter(s), :] = delta.astype(BF16)
        grad = dot(a1t[...], delta_s[1])
        for v in range(5):
            rows = pl.ds(64 * v + start, 16)
            fgrad_s[rows, :] = grad[16 * v : 16 * v + 16]
            vgrad_s[rows, :] = grad[80 + 16 * v : 96 + 16 * v]
        return carry

    lax.fori_loop(0, 4, group, 0, unroll=True)
    adj = adj_ref[...]
    total = (adj + vgrad_s[...]).astype(BF16)
    local = dot_first(volume_op_ref[...], total) + fgrad_s[...] + out_ref[...]
    out_ref[...] = 0.5 * cot_ref[...] + adj + STEP * local


def fifth_kernel(place_ref, table_ref, *refs):
    arrays, refs = refs[:7], refs[7:]
    (
        fin_part_ref, out_part_ref, partner_ref, dom_send_ref, dom_count_ref, sub_send_ref,
        lift_hi, lift_lo, back_hi, back_lo, fin_ref, out_ref, fin_s, out_s, sems,
    ) = refs
    nbr, back = arrived_parts(
        arrays, partner_ref[...], dom_send_ref[...], dom_count_ref[...], sub_send_ref[...],
        route_of(place_ref, table_ref), place_ref[0] >> 1, place_ref[1],
    )
    nbr_b = nbr.astype(BF16)
    fin_s[...] = fin_part_ref[...] + (0.5 * STEP) * (dot(lift_hi[...], nbr_b) + dot(lift_lo[...], nbr_b))
    moves = [pltpu.make_async_copy(fin_s, fin_ref, sems.at[0])]
    moves[0].start()
    for i in range(2):
        rows = slice(160 * i, 160 * i + 160)
        out_s[rows, :] = out_part_ref[rows, :] + STEP * lifted(back, back_hi[rows, :], back_lo[rows, :])
        moves.append(pltpu.make_async_copy(out_s.at[rows], out_ref.at[rows], sems.at[1 + i]))
        moves[-1].start()
    for move in moves:
        move.wait()


def call(kernel, name, outs, inputs, scratch=(), scalars=0, cost=None, final=False, raw=False):
    specs = [pl.BlockSpec(memory_space=pltpu.SMEM)] * scalars
    specs += [pl.BlockSpec(memory_space=pltpu.HBM if raw else pltpu.VMEM)] * (len(inputs) - scalars)
    kind = jax.ShapeDtypeStruct if final else pltpu.VMEM
    scratch = [pltpu.VMEM(shape, dtype) for shape, dtype in scratch]
    if scalars:
        inputs = (inputs[0], pltpu.with_memory_space_constraint(inputs[1], pltpu.HBM)) + tuple(inputs[2:])
    if raw:
        inputs = inputs[:scalars] + tuple(pltpu.with_memory_space_constraint(x, pltpu.HBM) for x in inputs[scalars:])
        scratch.append(pltpu.SemaphoreType.DMA((len(inputs) - scalars,)))
    if final:
        scratch.append(pltpu.SemaphoreType.DMA((3,)))
    return pl.pallas_call(
        kernel,
        name=name,
        out_shape=[kind(shape, dtype) for shape, dtype in outs],
        in_specs=specs,
        out_specs=[pl.BlockSpec(memory_space=pltpu.HBM if final else pltpu.VMEM)] * len(outs),
        scratch_shapes=scratch,
        cost_estimate=cost,
        compiler_params=pltpu.CompilerParams(vmem_limit_bytes=30 * 1024 * 1024),
    )(*inputs)


PAYLOAD = [((160, 128), BF16)] * 3 + [((2, 160, 128), BF16), ((160, 128), BF16)]
STATE = ((320, E), F32)
STATE_B = ((320, E), BF16)
MATRICES = [
    ((1024, 160), BF16), ((160, 1024), BF16), ((256, 256), BF16), ((256, 256), BF16),
    ((80, 1024), BF16), ((1024, 80), BF16),
    ((320, 480), BF16), ((320, 480), BF16), ((320, 480), BF16), ((320, 480), BF16), ((2, 256, 128), F32),
]
PAIR = ((2, 1024, E), BF16)
COST = pl.CostEstimate(flops=10_000_000_000, transcendentals=0, bytes_accessed=8_000_000)


def exchange(place, filler, same, cross, own, near, last):
    def hop(x, target):
        return lax.ppermute(x, "dom", [(d, target(d)) for d in range(N_DOM)])

    def swap(x, k):
        return lax.ppermute(x, "sub", [(i, i ^ k) for i in range(4)])

    core = hop(cross, to_core)
    near = swap(near, 1)
    core, near, filler = lax.optimization_barrier((core, near, filler))
    pair = hop(jnp.stack([same, core]), to_pair)
    last = swap(jnp.stack([last, near[1]]), 3)
    group = iota((160, 128), 1) // 32
    up = jnp.where(group == 0, same, jnp.where(group == 1, core, jnp.where(group == 2, pair[0], pair[1])))
    down = jnp.where(group == 0, core, jnp.where(group == 1, same, jnp.where(group == 2, pair[1], pair[0])))
    first = ((place[0] >> 2) & 1) == 0
    even = hop(jnp.where(first, up, down), reversed_even)
    odd = hop(jnp.where(first, down, up), reversed_odd)
    return filler, (core, pair, even, odd, own, near, last)


def body(
    initial_state, cotangent, volume_operator, in_weight, in_bias, mid_weight, mid_bias, out_weight, flux_matrix,
    dom_send, dom_count, sub_send, partner,
):
    select = jnp.asarray(face_select(), BF16)
    table = jnp.asarray(routing_tables().reshape(-1))
    place = jnp.stack([lax.axis_index("dom"), lax.axis_index("sub")]).astype(I32)
    raw = (
        initial_state, cotangent, select, partner, dom_send, dom_count, sub_send,
        volume_operator, in_weight.T, mid_weight, out_weight, flux_matrix, in_bias.reshape(1, 64), mid_bias.reshape(1, 64),
    )
    copies = [(x.shape, x.dtype) for x in raw]
    done = call(first_kernel, "first", copies + PAYLOAD, (place, table) + raw, scalars=2, raw=True)
    initial_state, cotangent, select, partner, dom_send, dom_count, sub_send, volume_operator = done[:8]
    lists = (partner, dom_send, dom_count, sub_send)
    mats = call(weights_kernel, "weights", MATRICES, tuple(done[8 : len(raw)]))
    mats, arrived = exchange(place, mats, *done[len(raw):])
    a1, a1t, wm, wmt, a3, a3t, lift_hi, lift_lo, back_hi, back_lo, bias = mats
    lifts = (lift_hi, lift_lo, back_hi, back_lo)
    part, adj_part, slope1, slope2 = call(
        second_kernel, "second", [STATE, STATE, ((4, 1024, E), BF16), ((4, 1024, E), BF16)],
        (initial_state, cotangent, select, partner, volume_operator, a1, wm, a3, *lifts, bias),
        [STATE_B, STATE_B, PAIR], cost=COST,
    )
    middle, base, adj, *sent = call(
        third_kernel, "third", [STATE, STATE, STATE] + PAYLOAD,
        (place, table, *arrived, part, adj_part, cotangent, select, *lists, volume_operator, *mats),
        [STATE_B, STATE_B, STATE_B, STATE, STATE, PAIR, ((1024, E), F32), PAIR], scalars=2,
    )
    fin_part = call(
        jump_kernel, "jump", [STATE], (initial_state, middle, base, select, partner, lift_hi, lift_lo)
    )
    fin_part, arrived = exchange(place, fin_part, *sent)
    out_part = call(
        fourth_kernel, "fourth", [STATE],
        (cotangent, adj, select, partner, volume_operator, slope1, slope2, a1t, wmt, a3t, back_hi, back_lo),
        [STATE_B, STATE, STATE, PAIR], cost=COST,
    )
    final_state, adjoint_state = call(
        fifth_kernel, "fifth", [STATE, STATE],
        (place, table, *arrived, *fin_part, *out_part, *lists, *lifts), [STATE, STATE], scalars=2, final=True,
    )
    return final_state, adjoint_state


def solution(mesh):
    columns = P(None, ("dom", "sub"))
    pairs = P("dom", "sub")
    return jax.shard_map(
        body,
        mesh=mesh,
        in_specs=(columns, columns, P(), P(), P(), P(), P(), P(), P(), pairs, pairs, pairs, pairs),
        out_specs=(columns, columns),
        check_vma=False,
    )
```

```python
import jax
import jax.numpy as jnp
import numpy as np
from jax import lax
from jax.experimental import pallas as pl
from jax.experimental.pallas import tpu as pltpu
from jax.sharding import PartitionSpec as P

E = 256
LOCAL = 6 * E
OFFSETS = (-4, -3, -2, -1, 1, 2, 3, 4)
N_DOM = 64
STEP = 0.4
GAIN = 1.5
F32, BF16, I32 = jnp.float32, jnp.bfloat16, jnp.int32


def block_of(offset):
    return OFFSETS.index(offset)


def to_core(d):
    return d ^ 1


def to_pair(d):
    return d ^ 2


def reversed_even(d):
    return d ^ 6


def reversed_odd(d):
    chip, core = divmod(d, 2)
    other = ((chip + 2) ^ 3) - 2
    return 2 * other + core if 0 <= other < N_DOM // 2 else d


def sent_offsets(d):
    return (2, -2, 4, -4) + ((-3, 1, -1, 3) if d % 2 else (-1, 3, -3, 1))


def routing_tables():
    hold = {d: [(d, o) for o in sent_offsets(d)] for d in range(N_DOM)}
    core = {d: hold[to_core(d)][4:] for d in range(N_DOM)}
    even, odd, direct = {}, {}, {}
    for d in range(N_DOM):
        same, other = hold[to_pair(d)][:4], core[to_pair(d)]
        up = [hold[d][0], core[d][1], same[2], other[3]]
        down = [core[d][0], hold[d][1], other[2], same[3]]
        even[d], odd[d] = (down, up) if d // 4 % 2 else (up, down)
        direct[d] = ([same[0], other[1]] if d // 2 % 2 else [other[0], same[1]]) + core[d][2:]
    rows = []
    for d in range(N_DOM):
        found = direct[d] + even[reversed_even(d)] + odd[reversed_odd(d)]
        arrived = [None] * 12
        for i, item in enumerate(found):
            if item[0] != d and sum(item) == d and item[1] not in arrived:
                arrived[i] = item[1]
        wanted = [o for o in OFFSETS if 0 <= d - o < N_DOM]
        assert sorted(o for o in arrived if o is not None) == wanted
        sent = sent_offsets(d)
        assert sorted(sent) == list(OFFSETS)
        row = [block_of(o) for o in sent]
        row += [sent.index(-o) for o in OFFSETS]
        row += [-1 if o is None else block_of(-o) for o in arrived]
        row += [arrived.index(o) if o in arrived else -1 for o in OFFSETS]
        rows.append(row)
    return np.array(rows, np.int32)


SENT_BLOCK, SENT_PLACE, ARRIVED_BLOCK, ARRIVED_PLACE, TABLE_WIDTH = 0, 8, 16, 28, 36


def face_nodes():
    nodes = np.zeros((6, 16), np.int32)
    for k in range(16):
        hi, lo = divmod(k, 4)
        nodes[:, k] = (4 * lo + 16 * hi, 3 + 4 * lo + 16 * hi, lo + 16 * hi, 12 + lo + 16 * hi, k, 48 + k)
    return nodes


def face_select():
    nodes = face_nodes()
    select = np.zeros((480, 320), np.float32)
    for f in range(6):
        for v in range(5):
            for k in range(16):
                select[f * 80 + v * 16 + k, v * 64 + nodes[f, k]] = 1.0
    return select


def dot(a, b):
    return lax.dot_general(a, b, (((1,), (0,)), ((), ())), preferred_element_type=F32)


def dot_t(a, b):
    return lax.dot_general(a, b, (((1,), (1,)), ((), ())), preferred_element_type=F32)


def dot_first(a, b):
    return lax.dot_general(a, b, (((0,), (0,)), ((), ())), preferred_element_type=F32)


def iota(shape, dim):
    return lax.broadcasted_iota(I32, shape, dim)


def as_one(mask):
    return jnp.where(mask, 1.0, 0.0)


def split(x):
    hi = x.astype(BF16)
    return hi, (x - hi.astype(F32)).astype(BF16)


def dom_labels(dom_send, dom_count, blocks):
    width = 32 * len(blocks)
    slots = iota((8, E), 1)
    spread = as_one(iota((8, E), 0) == slots // 32).astype(BF16)
    counts = dot(jnp.broadcast_to(dom_count.astype(F32), (8, 8)).astype(BF16), spread)
    live = as_one((slots % 32).astype(F32) < counts)
    lists = jnp.broadcast_to(dom_send, (8, E))
    row = iota((8, E), 0)
    table = jnp.where(row == 0, (lists // 256).astype(F32), jnp.where(row == 1, (lists % 256).astype(F32), 1.0))
    table = (table * live).astype(BF16)
    lanes = iota((8, width), 1)
    source = jnp.full(lanes.shape, -1, I32)
    for i, block in enumerate(blocks):
        source = jnp.where(lanes >> 5 == i, block, source)
    source = jnp.where(source >= 0, source * 32 + (lanes & 31), -1)
    pick = as_one(iota((E, width), 0) == source[0:1, :]).astype(BF16)
    found = dot(table, pick)
    label = jnp.where(found[2:3] > 0.5, found[0:1] * 256.0 + found[1:2], -1.0)
    return label.astype(I32)


def sub_labels(sub_send, sub):
    blocks = [sub_send[:, 128 * t : 128 * t + 128] for t in range(4)]
    result = []
    for k in range(4):
        block = blocks[k]
        for s in range(1, 4):
            block = jnp.where(sub == s, blocks[s ^ k], block)
        result.append(block)
    return result


def source_rows(partner, sub, places, width):
    received = partner - LOCAL
    block = received >> 5
    place = jnp.full(partner.shape, -32, I32)
    for j, group in enumerate(places):
        place = jnp.where(block == j, 32 * group, place)
    place = place + (received & 31)
    over = received - E
    over = width + (((over >> 7) ^ sub) << 7) + (over & 127)
    return jnp.where(received >= E, over, jnp.where(received >= 0, place, -1))


def low_hot(row):
    column = iota((E, 128), 0)
    parts = [as_one(column == (row[:, i : i + 128] & 255)) for i in range(0, row.shape[1], 128)]
    return jnp.concatenate(parts, axis=1).astype(BF16)


def gather(blocks, row, count):
    rows = blocks.shape[0] // count
    out = []
    for start in range(0, row.shape[1], 256):
        part = row[:, start : start + 256]
        found = dot(blocks, low_hot(part))
        taken = jnp.zeros((rows, part.shape[1]), F32)
        for b in range(count):
            taken = jnp.where(part >> 8 == b, found[rows * b : rows * b + rows], taken)
        out.append(taken)
    return out


def scatter(values, row, count):
    block = row >> 8
    spread = [values * as_one(block == b).astype(BF16) for b in range(count)]
    return dot_t(jnp.concatenate(spread, axis=0), low_hot(row))


def payload_plan(partner, dom_send, dom_count, sub_send, route, sub):
    labels = dom_labels(dom_send, dom_count, route(SENT_BLOCK, 8))
    labels = jnp.concatenate([labels] + sub_labels(sub_send, sub), axis=1)
    return labels, source_rows(partner, sub, route(SENT_PLACE, 8), E)


def payload(field_b, g_hi, select_ref, plan, outs):
    labels, places = plan
    traces = dot(select_ref[...], field_b).astype(BF16)
    owed = dot(select_ref[...], g_hi).astype(BF16)
    owed = jnp.concatenate([owed[80 * f : 80 * f + 80] for f in range(6)], axis=1)
    sent = jnp.concatenate(gather(traces, labels, 6), axis=1).astype(BF16)
    back = scatter(owed, places, 3).astype(BF16)
    same_ref, cross_ref, own_ref, near_ref, last_ref = outs
    for i, ref in enumerate((same_ref, cross_ref, own_ref, near_ref.at[0], near_ref.at[1], last_ref)):
        ref[0:80, :] = sent[:, 128 * i : 128 * i + 128]
        b, half = divmod(i, 2)
        ref[80:160, :] = back[80 * b : 80 * b + 80, 128 * half : 128 * half + 128]


def lifted(faces, lift_hi, lift_lo):
    hi, lo = split(faces)
    return dot(lift_hi, hi) + dot(lift_hi, lo) + dot(lift_lo, hi)


def arrived_parts(arrays, partner, dom_send, dom_count, sub_send, route, chip, sub):
    core_ref, pair_ref, even_ref, odd_ref, own_ref, near_ref, last_ref = arrays
    group = iota((160, 128), 1) // 32
    direct = jnp.where(group == 1 - chip % 2, pair_ref[0], jnp.where(group < 2, pair_ref[1], core_ref[...]))
    parts = [direct, even_ref[...], odd_ref[...], own_ref[...], near_ref[0], last_ref[1], last_ref[0]]
    traces = [jnp.concatenate([parts[2 * b][0:80], parts[min(2 * b + 1, 6)][0:80]], axis=1) for b in range(4)]
    places = source_rows(partner, sub, route(ARRIVED_PLACE, 8), 384)
    nbr = jnp.concatenate(gather(jnp.concatenate(traces, axis=0), places, 4), axis=0)
    labels = dom_labels(dom_send, dom_count, route(ARRIVED_BLOCK, 12))
    labels = jnp.concatenate([labels] + sub_labels(sub_send, sub), axis=1)
    returned = jnp.concatenate([part[80:160] for part in parts], axis=1)
    return nbr, scatter(returned, labels, 6)


def local_jump(field_b, select_ref, partner):
    traces = dot(select_ref[...], field_b)
    return jnp.concatenate(gather(traces.astype(BF16), partner, 6), axis=0) - traces


def local_trace(g, select_ref, partner):
    select = select_ref[...]
    g_hi, g_lo = split(g)
    owed_hi, owed_lo = dot(select, g_hi), dot(select, g_lo)
    pair = jnp.concatenate(
        [jnp.concatenate([owed_hi[80 * f : 80 * f + 80], owed_lo[80 * f : 80 * f + 80]], axis=0) for f in range(6)],
        axis=1,
    ).astype(BF16)
    back = scatter(pair, partner, 6)
    back = jnp.concatenate([back[160 * f : 160 * f + 80] + back[160 * f + 80 : 160 * f + 160] for f in range(6)], axis=0)
    return back - (owed_hi + owed_lo)


def local_parts(field_b, g, select_ref, partner):
    select = select_ref[...]
    traces = dot(select, field_b)
    g_hi, g_lo = split(g)
    owed_hi, owed_lo = dot(select, g_hi), dot(select, g_lo)
    pair = jnp.concatenate(
        [jnp.concatenate([owed_hi[80 * f : 80 * f + 80], owed_lo[80 * f : 80 * f + 80]], axis=0) for f in range(6)],
        axis=1,
    ).astype(BF16)
    nbr = jnp.concatenate(gather(traces.astype(BF16), partner, 6), axis=0)
    back = scatter(pair, partner, 6)
    back = jnp.concatenate([back[160 * f : 160 * f + 80] + back[160 * f + 80 : 160 * f + 160] for f in range(6)], axis=0)
    return nbr - traces, back - (owed_hi + owed_lo)


def build_weights(in_t, mid_weight, out_weight, flux, biases, outs):
    a1, a1t, wm, wmt, a3, a3t, lift_hi, lift_lo, back_hi, back_lo, bias_ref = outs

    def mask(shape, condition, dtype=BF16):
        return as_one(condition(iota(shape, 0), iota(shape, 1))).astype(dtype)

    spread = mask((256, 64), lambda r, c: r // 4 == c)
    spread_t = mask((64, 256), lambda r, c: c // 4 == r)
    same = mask((256, 256), lambda r, c: r % 4 == c % 4, F32)
    wm[...] = (dot(dot(spread, mid_weight).astype(BF16), spread_t) * same).astype(BF16)
    wmt[...] = (dot(dot_t(spread, mid_weight).astype(BF16), spread_t) * same).astype(BF16)
    ten = mask((10, 160), lambda r, c: c // 16 == r)
    ten_t = mask((160, 10), lambda r, c: r // 16 == c)
    five = mask((5, 80), lambda r, c: c // 16 == r)
    five_t = mask((80, 5), lambda r, c: r // 16 == c)
    rows_in = dot(dot_t(spread, in_t).astype(BF16), ten)
    cols_in = dot(dot(ten_t, in_t).astype(BF16), spread_t)
    cols_out = dot(dot(five_t, out_weight).astype(BF16), spread_t)
    rows_out = dot(dot_t(spread, out_weight).astype(BF16), five)
    for s in range(4):
        a1[256 * s : 256 * s + 256, :] = (
            rows_in * mask((256, 160), lambda r, c: c % 16 == 4 * s + r % 4, F32)
        ).astype(BF16)
        a1t[:, 256 * s : 256 * s + 256] = (
            cols_in * mask((160, 256), lambda r, c: r % 16 == 4 * s + c % 4, F32)
        ).astype(BF16)
        a3[:, 256 * s : 256 * s + 256] = (
            cols_out * mask((80, 256), lambda r, c: r % 16 == 4 * s + c % 4, F32)
        ).astype(BF16)
        a3t[256 * s : 256 * s + 256, :] = (
            rows_out * mask((256, 80), lambda r, c: c % 16 == 4 * s + r % 4, F32)
        ).astype(BF16)
    ones = jnp.ones((64, 128), BF16)
    for i, bias in enumerate(biases):
        hi, _ = split(bias)
        mid, low = split(bias - hi.astype(F32))
        bias_ref[i] = dot(spread * hi, ones) + dot(spread * mid, ones) + dot(spread * low, ones)
    lane = iota((8, 480), 1)
    f, k = lane // 80, lane % 16
    hi, lo = k // 4, k % 4
    node = jnp.where(f < 2, 4 * lo + 16 * hi + 3 * f, jnp.where(f < 4, lo + 16 * hi + 12 * (f - 2), k + 48 * (f - 4)))
    meets = as_one(iota((320, 480), 0) % 64 == node[0:1])
    var = mask((320, 5), lambda r, c: r // 64 == c)
    var_t = mask((5, 480), lambda r, c: (c % 80) // 16 == r)
    for part, forward, backward in zip(split(GAIN * flux), (lift_hi, lift_lo), (back_hi, back_lo)):
        forward[...] = (dot(dot(var, part).astype(BF16), var_t) * meets).astype(BF16)
        backward[...] = (dot(dot_t(var, part).astype(BF16), var_t) * meets).astype(BF16)


def wide(bias):
    return jnp.concatenate([bias, bias], axis=1)


def quarter(s):
    return slice(256 * s, 256 * s + 256)


def group_rows(ref, start):
    return jnp.concatenate([ref[pl.ds(64 * v + start, 16), :] for v in range(5)], axis=0)


def group_inputs(field_ref, volume_ref, start):
    return jnp.concatenate([group_rows(field_ref, start), group_rows(volume_ref, start)], axis=0)


def route_of(place_ref, table_ref):
    row = place_ref[0] * TABLE_WIDTH

    def route(start, count):
        return [table_ref[row + start + i] for i in range(count)]

    return route


def first_kernel(place_ref, table_ref, *refs):
    count = (len(refs) - 6) // 2
    sources, copies, sems = refs[:count], refs[count : 2 * count], refs[-1]
    outs = refs[2 * count : -1]
    moves = [pltpu.make_async_copy(a, b, sems.at[i]) for i, (a, b) in enumerate(zip(sources, copies))]
    for move in moves:
        move.start()
    init_ref, cot_ref, select_ref, partner_ref, dom_send_ref, dom_count_ref, sub_send_ref = copies[:7]
    for move in moves[3:7]:
        move.wait()
    route, sub = route_of(place_ref, table_ref), place_ref[1]
    plan = payload_plan(partner_ref[...], dom_send_ref[...], dom_count_ref[...], sub_send_ref[...], route, sub)
    for move in moves[:3]:
        move.wait()
    payload(init_ref[...].astype(BF16), cot_ref[...].astype(BF16), select_ref, plan, outs)
    for move in moves[7:]:
        move.wait()


def weights_kernel(in_ref, mid_ref, out_ref, flux_ref, in_bias_ref, mid_bias_ref, *outs):
    build_weights(in_ref[...], mid_ref[...], out_ref[...], flux_ref[...], (in_bias_ref[...], mid_bias_ref[...]), outs)


def second_kernel(
    init_ref, cot_ref, select_ref, partner_ref, volume_op_ref, a1, wm, a3, lift_hi, lift_lo, back_hi, back_lo, bias_ref,
    part_ref, adj_ref, slope1_ref, slope2_ref, field_s, volume_s, h_s,
):
    field_b = init_ref[...].astype(BF16)
    jump, trace_grad = local_parts(field_b, cot_ref[...], select_ref, partner_ref[...])
    adj_ref[...] = 0.5 * cot_ref[...] + (0.5 * STEP) * lifted(trace_grad, back_hi[...], back_lo[...])
    volume = dot(volume_op_ref[...], field_b)
    part_ref[...] = init_ref[...] + STEP * (volume + lifted(jump, lift_hi[...], lift_lo[...]))
    field_s[...] = field_b
    volume_s[...] = volume.astype(BF16)

    def group(i, carry):
        start = pl.multiple_of(16 * i, 16)
        inputs = group_inputs(field_s, volume_s, start)
        for s in range(4):
            h1 = jnp.tanh(dot(a1[quarter(s), :], inputs) + wide(bias_ref[0]))
            h_s[0, quarter(s), :] = h1.astype(BF16)
            slope1_ref[i, quarter(s), :] = (1.0 - h1 * h1).astype(BF16)
        for s in range(4):
            h2 = jnp.tanh(dot(wm[...], h_s[0, quarter(s), :]) + wide(bias_ref[1]))
            h_s[1, quarter(s), :] = h2.astype(BF16)
            slope2_ref[i, quarter(s), :] = (1.0 - h2 * h2).astype(BF16)
        out = dot(a3[...], h_s[1])
        for v in range(5):
            rows = pl.ds(64 * v + start, 16)
            part_ref[rows, :] = part_ref[rows, :] + STEP * out[16 * v : 16 * v + 16]
        return carry

    lax.fori_loop(0, 4, group, 0)


def third_kernel(place_ref, table_ref, *refs):
    arrays, refs = refs[:7], refs[7:]
    (
        part_ref, adj_part_ref, cot_ref, select_ref, partner_ref,
        dom_send_ref, dom_count_ref, sub_send_ref, volume_op_ref,
        a1, a1t, wm, wmt, a3, a3t, lift_hi, lift_lo, back_hi, back_lo, bias_ref,
        middle_ref, base_ref, adj_ref, *sent_refs,
    ) = refs[:28]
    field_s, volume_s, cot_s, fgrad_s, vgrad_s, h_s, slope_s, delta_s = refs[28:]
    route, sub = route_of(place_ref, table_ref), place_ref[1]
    partner, dom_send, dom_count, sub_send = partner_ref[...], dom_send_ref[...], dom_count_ref[...], sub_send_ref[...]
    nbr, back = arrived_parts(arrays, partner, dom_send, dom_count, sub_send, route, place_ref[0] >> 1, sub)
    nbr_b = nbr.astype(BF16)
    middle = part_ref[...] + STEP * (dot(lift_hi[...], nbr_b) + dot(lift_lo[...], nbr_b))
    middle_ref[...] = middle
    adj_ref[...] = adj_part_ref[...] + (0.5 * STEP) * lifted(back, back_hi[...], back_lo[...])
    field_b = middle.astype(BF16)
    volume = dot(volume_op_ref[...], field_b)
    base_ref[...] = volume
    field_s[...] = field_b
    volume_s[...] = volume.astype(BF16)
    cot_s[...] = cot_ref[...].astype(BF16)

    def group(i, carry):
        start = pl.multiple_of(16 * i, 16)
        inputs = group_inputs(field_s, volume_s, start)
        upstream = group_rows(cot_s, start)
        for s in range(4):
            h1 = jnp.tanh(dot(a1[quarter(s), :], inputs) + wide(bias_ref[0]))
            h_s[0, quarter(s), :] = h1.astype(BF16)
            slope_s[quarter(s), :] = 1.0 - h1 * h1
        for s in range(4):
            h2 = jnp.tanh(dot(wm[...], h_s[0, quarter(s), :]) + wide(bias_ref[1]))
            h_s[1, quarter(s), :] = h2.astype(BF16)
            delta_s[0, quarter(s), :] = (dot(a3t[quarter(s), :], upstream) * (1.0 - h2 * h2)).astype(BF16)
        out = dot(a3[...], h_s[1])
        for s in range(4):
            delta_s[1, quarter(s), :] = (dot(wmt[...], delta_s[0, quarter(s), :]) * slope_s[quarter(s), :]).astype(BF16)
        grad = dot(a1t[...], delta_s[1])
        for v in range(5):
            rows = pl.ds(64 * v + start, 16)
            base_ref[rows, :] = base_ref[rows, :] + out[16 * v : 16 * v + 16]
            fgrad_s[rows, :] = grad[16 * v : 16 * v + 16]
            vgrad_s[rows, :] = grad[80 + 16 * v : 96 + 16 * v]
        return carry

    lax.fori_loop(0, 4, group, 0, unroll=True)
    total = (cot_ref[...] + vgrad_s[...]).astype(BF16)
    adj = adj_ref[...] + (0.5 * STEP) * (dot_first(volume_op_ref[...], total) + fgrad_s[...])
    adj_ref[...] = adj
    plan = payload_plan(partner, dom_send, dom_count, sub_send, route, sub)
    payload(field_b, adj.astype(BF16), select_ref, plan, sent_refs)


def jump_kernel(init_ref, middle_ref, base_ref, select_ref, partner_ref, lift_hi, lift_lo, fin_ref):
    middle = middle_ref[...]
    jump = local_jump(middle.astype(BF16), select_ref, partner_ref[...])
    residual = base_ref[...] + lifted(jump, lift_hi[...], lift_lo[...])
    fin_ref[...] = 0.5 * init_ref[...] + 0.5 * (middle + STEP * residual)


def fourth_kernel(
    cot_ref, adj_ref, select_ref, partner_ref, volume_op_ref, slope1_ref, slope2_ref, a1t, wmt, a3t, back_hi, back_lo,
    out_ref, adj_s, fgrad_s, vgrad_s, delta_s,
):
    adj = adj_ref[...]
    trace_grad = local_trace(adj, select_ref, partner_ref[...])
    out_ref[...] = lifted(trace_grad, back_hi[...], back_lo[...])
    adj_s[...] = adj.astype(BF16)

    def group(i, carry):
        start = pl.multiple_of(16 * i, 16)
        upstream = group_rows(adj_s, start)
        for s in range(4):
            delta = dot(a3t[quarter(s), :], upstream) * slope2_ref[i, quarter(s), :].astype(F32)
            delta_s[0, quarter(s), :] = delta.astype(BF16)
        for s in range(4):
            delta = dot(wmt[...], delta_s[0, quarter(s), :]) * slope1_ref[i, quarter(s), :].astype(F32)
            delta_s[1, quarter(s), :] = delta.astype(BF16)
        grad = dot(a1t[...], delta_s[1])
        for v in range(5):
            rows = pl.ds(64 * v + start, 16)
            fgrad_s[rows, :] = grad[16 * v : 16 * v + 16]
            vgrad_s[rows, :] = grad[80 + 16 * v : 96 + 16 * v]
        return carry

    lax.fori_loop(0, 4, group, 0, unroll=True)
    adj = adj_ref[...]
    total = (adj + vgrad_s[...]).astype(BF16)
    local = dot_first(volume_op_ref[...], total) + fgrad_s[...] + out_ref[...]
    out_ref[...] = 0.5 * cot_ref[...] + adj + STEP * local


def fifth_kernel(place_ref, table_ref, *refs):
    arrays, refs = refs[:7], refs[7:]
    (
        fin_part_ref, out_part_ref, partner_ref, dom_send_ref, dom_count_ref, sub_send_ref,
        lift_hi, lift_lo, back_hi, back_lo, fin_ref, out_ref, fin_s, out_s, sems,
    ) = refs
    nbr, back = arrived_parts(
        arrays, partner_ref[...], dom_send_ref[...], dom_count_ref[...], sub_send_ref[...],
        route_of(place_ref, table_ref), place_ref[0] >> 1, place_ref[1],
    )
    nbr_b = nbr.astype(BF16)
    fin_s[...] = fin_part_ref[...] + (0.5 * STEP) * (dot(lift_hi[...], nbr_b) + dot(lift_lo[...], nbr_b))
    moves = [pltpu.make_async_copy(fin_s, fin_ref, sems.at[0])]
    moves[0].start()
    for i in range(2):
        rows = slice(160 * i, 160 * i + 160)
        out_s[rows, :] = out_part_ref[rows, :] + STEP * lifted(back, back_hi[rows, :], back_lo[rows, :])
        moves.append(pltpu.make_async_copy(out_s.at[rows], out_ref.at[rows], sems.at[1 + i]))
        moves[-1].start()
    for move in moves:
        move.wait()


def call(kernel, outs, inputs, scratch=(), scalars=0, cost=None, final=False, raw=False):
    specs = [pl.BlockSpec(memory_space=pltpu.SMEM)] * scalars
    specs += [pl.BlockSpec(memory_space=pltpu.HBM if raw else pltpu.VMEM)] * (len(inputs) - scalars)
    kind = jax.ShapeDtypeStruct if final else pltpu.VMEM
    scratch = [pltpu.VMEM(shape, dtype) for shape, dtype in scratch]
    if scalars:
        inputs = (inputs[0], pltpu.with_memory_space_constraint(inputs[1], pltpu.HBM)) + tuple(inputs[2:])
    if raw:
        inputs = inputs[:scalars] + tuple(pltpu.with_memory_space_constraint(x, pltpu.HBM) for x in inputs[scalars:])
        scratch.append(pltpu.SemaphoreType.DMA((len(inputs) - scalars,)))
    if final:
        scratch.append(pltpu.SemaphoreType.DMA((3,)))
    return pl.pallas_call(
        kernel,
        out_shape=[kind(shape, dtype) for shape, dtype in outs],
        in_specs=specs,
        out_specs=[pl.BlockSpec(memory_space=pltpu.HBM if final else pltpu.VMEM)] * len(outs),
        scratch_shapes=scratch,
        cost_estimate=cost,
        compiler_params=pltpu.CompilerParams(vmem_limit_bytes=30 * 1024 * 1024),
    )(*inputs)


PAYLOAD = [((160, 128), BF16)] * 3 + [((2, 160, 128), BF16), ((160, 128), BF16)]
STATE = ((320, E), F32)
STATE_B = ((320, E), BF16)
MATRICES = [
    ((1024, 160), BF16), ((160, 1024), BF16), ((256, 256), BF16), ((256, 256), BF16),
    ((80, 1024), BF16), ((1024, 80), BF16),
    ((320, 480), BF16), ((320, 480), BF16), ((320, 480), BF16), ((320, 480), BF16), ((2, 256, 128), F32),
]
PAIR = ((2, 1024, E), BF16)
COST = pl.CostEstimate(flops=10_000_000_000, transcendentals=0, bytes_accessed=8_000_000)


def exchange(place, same, cross, own, near, last, fill):
    def hop(x, target):
        return lax.ppermute(x, "dom", [(d, target(d)) for d in range(N_DOM)])

    def swap(x, k):
        return lax.ppermute(x, "sub", [(i, i ^ k) for i in range(4)])

    core = hop(cross, to_core)
    near = swap(near, 1)
    pair = hop(jnp.stack([same, core]), to_pair)
    filled = fill()
    pair, filled = lax.optimization_barrier((pair, filled))
    last = swap(jnp.stack([last, near[1]]), 3)
    group = iota((160, 128), 1) // 32
    up = jnp.where(group == 0, same, jnp.where(group == 1, core, jnp.where(group == 2, pair[0], pair[1])))
    down = jnp.where(group == 0, core, jnp.where(group == 1, same, jnp.where(group == 2, pair[1], pair[0])))
    first = ((place[0] >> 2) & 1) == 0
    even = hop(jnp.where(first, up, down), reversed_even)
    odd = hop(jnp.where(first, down, up), reversed_odd)
    return filled, (core, pair, even, odd, own, near, last)


def body(
    initial_state, cotangent, volume_operator, in_weight, in_bias, mid_weight, mid_bias, out_weight, flux_matrix,
    dom_send, dom_count, sub_send, partner,
):
    select = jnp.asarray(face_select(), BF16)
    table = jnp.asarray(routing_tables().reshape(-1))
    place = jnp.stack([lax.axis_index("dom"), lax.axis_index("sub")]).astype(I32)
    raw = (
        initial_state, cotangent, select, partner, dom_send, dom_count, sub_send,
        volume_operator, in_weight.T, mid_weight, out_weight, flux_matrix, in_bias.reshape(1, 64), mid_bias.reshape(1, 64),
    )
    copies = [(x.shape, x.dtype) for x in raw]
    done = call(first_kernel, copies + PAYLOAD, (place, table) + raw, scalars=2, raw=True)
    initial_state, cotangent, select, partner, dom_send, dom_count, sub_send, volume_operator = done[:8]
    lists = (partner, dom_send, dom_count, sub_send)
    mats, arrived = exchange(place, *done[len(raw):], lambda: call(weights_kernel, MATRICES, tuple(done[8 : len(raw)])))
    a1, a1t, wm, wmt, a3, a3t, lift_hi, lift_lo, back_hi, back_lo, bias = mats
    lifts = (lift_hi, lift_lo, back_hi, back_lo)
    part, adj_part, slope1, slope2 = call(
        second_kernel, [STATE, STATE, ((4, 1024, E), BF16), ((4, 1024, E), BF16)],
        (initial_state, cotangent, select, partner, volume_operator, a1, wm, a3, *lifts, bias),
        [STATE_B, STATE_B, PAIR], cost=COST,
    )
    middle, base, adj, *sent = call(
        third_kernel, [STATE, STATE, STATE] + PAYLOAD,
        (place, table, *arrived, part, adj_part, cotangent, select, *lists, volume_operator, *mats),
        [STATE_B, STATE_B, STATE_B, STATE, STATE, PAIR, ((1024, E), F32), PAIR], scalars=2,
    )
    fin_part, arrived = exchange(
        place, *sent,
        lambda: call(jump_kernel, [STATE], (initial_state, middle, base, select, partner, lift_hi, lift_lo)),
    )
    out_part = call(
        fourth_kernel, [STATE],
        (cotangent, adj, select, partner, volume_operator, slope1, slope2, a1t, wmt, a3t, back_hi, back_lo),
        [STATE_B, STATE, STATE, PAIR], cost=COST,
    )
    final_state, adjoint_state = call(
        fifth_kernel, [STATE, STATE],
        (place, table, *arrived, *fin_part, *out_part, *lists, *lifts), [STATE, STATE], scalars=2, final=True,
    )
    return final_state, adjoint_state


def solution(mesh):
    columns = P(None, ("dom", "sub"))
    pairs = P("dom", "sub")
    return jax.shard_map(
        body,
        mesh=mesh,
        in_specs=(columns, columns, P(), P(), P(), P(), P(), P(), P(), pairs, pairs, pairs, pairs),
        out_specs=(columns, columns),
        check_vma=False,
    )
```
